1024 devices in a mesh: ctx: 32 (over z), exp: 4 (over x), tp: 8 (over y, core).
Axes of the slice: x: 4, y: 4, z: 32, core: 2. Of those that a mesh axis runs over, the one named last changes fastest.
Arguments:
- queries: bfloat16 [65536, 4096], P(('ctx', 'exp'), 'tp'), may hold values from -6 to 6
- key_vectors: bfloat16 [65536, 4096], P(('ctx', 'exp'), 'tp'), may hold values from -6 to 6
- value_vectors: bfloat16 [65536, 4096], P(('ctx', 'exp'), 'tp'), may hold values from -6 to 6
- decay_rate: float32 [32], P('tp'), may hold values from 1e-07 to 0.05
- norm_gain: float32 [4096], P('tp'), may hold values from 0.5 to 1.5
Outputs:
- normed: bfloat16 [65536, 4096], P(('ctx', 'exp'), 'tp')
The draws below stay inside these ranges and needn't reach their ends.
All inputs are finite; a program needn't handle non-finite values.
Results may differ from the reference program's by a relative error of at most 0.0052.
Values sent between devices are 32-bit elements; how exact they have to be, the bound alone decides.
A program may use at most 128 MiB of HBM per device.

```python
import math
import jax
import jax.numpy as jnp
from jax import lax

HEADS = 32
HEAD_DIM = 128
BLK = 256
SEQ = 65536


def steps_of(key, shape, cuts, smallest, high):
    def one(axis_at, parts):
        heights = jax.random.uniform(jax.random.fold_in(jax.random.fold_in(key, 6), axis_at), (parts,), jnp.float32, smallest / len(cuts), high / len(cuts))
        return jnp.repeat(jnp.exp(heights), shape[axis_at] // parts).reshape((-1,) + (1,) * (len(shape) - axis_at - 1))

    level = one(*cuts[0])
    for cut in cuts[1:]:
        level = level * one(*cut)
    return level


def normal_values(rng, extent, scale, limit, split=(), held_as=jnp.bfloat16):
    loudness = steps_of(rng, extent, split, -0.22, 0.18) if split else 1.0
    entries = jax.random.normal(rng, extent, jnp.float32) * scale * loudness
    return jnp.minimum(jnp.maximum(entries, -limit), limit).astype(held_as)


def setup_inputs(seed: int = 0) -> dict:
    arg_keys = jax.random.split(jax.random.key(seed), 6)
    return {
        "queries": normal_values(arg_keys[0], (SEQ, HEADS * HEAD_DIM), 1.0, 6.0, ((0, 128), (1, 8))),
        "key_vectors": normal_values(arg_keys[1], (SEQ, HEADS * HEAD_DIM), 1.0, 6.0, ((0, 128), (1, 8))),
        "value_vectors": normal_values(arg_keys[2], (SEQ, HEADS * HEAD_DIM), 1.0, 6.0, ((0, 128), (1, 8))),
        "decay_rate": jnp.clip(jnp.exp(math.log(0.05) - 13.122363 * jax.random.uniform(arg_keys[3], (HEADS,), jnp.float32) ** steps_of(arg_keys[3], (HEADS,), ((0, 8),), -0.2, 0.2)), 1.0000000116860974e-07, 0.05),
        "norm_gain": jnp.clip(1.0 + 0.1 * jax.random.normal(arg_keys[4], (HEADS * HEAD_DIM,), jnp.float32), 0.5, 1.5),
    }


def reference(queries, key_vectors, value_vectors, decay_rate, norm_gain):
    seq_len = queries.shape[0]
    blocks = seq_len // BLK
    query_blocks = queries.reshape(blocks, BLK, HEADS, HEAD_DIM)
    key_blocks = key_vectors.reshape(blocks, BLK, HEADS, HEAD_DIM)
    value_blocks = value_vectors.reshape(blocks, BLK, HEADS, HEAD_DIM)
    offsets = jnp.arange(BLK, dtype=jnp.float32)
    spread = offsets[:, None] - offsets[None, :]
    causal = spread >= 0
    rates = decay_rate[:, None, None]
    weight = jnp.where(causal[None], jnp.exp(-rates * jnp.maximum(spread, 0.0)[None]), 0.0)
    inner_decay = jnp.exp(-decay_rate[None, :] * offsets[:, None])
    tail_decay = jnp.exp(-decay_rate[None, :] * (BLK - offsets)[:, None])
    block_decay = jnp.exp(-decay_rate * BLK)[:, None, None]

    def advance(carry_state, block_data):
        query_block, key_block, value_block = block_data
        query_wide = query_block.astype(jnp.float32)
        value_wide = value_block.astype(jnp.float32)
        scores = jnp.einsum('thd,shd->hts', query_wide, key_block.astype(jnp.float32))
        mixing = (scores * weight).astype(jnp.bfloat16)
        local_part = jnp.einsum('hts,she->the', mixing.astype(jnp.float32), value_wide)
        state_low = lax.optimization_barrier(carry_state.astype(jnp.bfloat16))
        carried = jnp.einsum('thd,hde->the', query_wide, state_low.astype(jnp.float32)) * inner_decay[:, :, None]
        scaled_keys = (key_block.astype(jnp.float32) * tail_decay[:, :, None]).astype(jnp.bfloat16)
        block_term = jnp.einsum('shd,she->hde', scaled_keys.astype(jnp.float32), value_wide)
        return (block_decay * carry_state + block_term, local_part + carried)
    start_state = jnp.zeros((HEADS, HEAD_DIM, HEAD_DIM), jnp.float32)
    unused, attended = lax.scan(advance, start_state, (query_blocks, key_blocks, value_blocks))
    attended = attended.reshape(seq_len, HEADS * HEAD_DIM)
    mean_square = lax.optimization_barrier(jnp.mean(attended * attended, axis=1, keepdims=True))
    normed = attended * lax.rsqrt(mean_square + 1e-06) * norm_gain[None, :]
    return normed.astype(jnp.bfloat16)
```

```python
import functools

import jax
import jax.numpy as jnp
from jax import lax
from jax.experimental import pallas as pl
from jax.experimental.pallas import tpu as pltpu
from jax.sharding import PartitionSpec as P

HEADS = 32
HEAD_DIM = 128
BLK = 256
GROUP = 4
MESH = pl.DeviceIdType.MESH


def kernel(
    sizes,
    q_hbm,
    k_hbm,
    v_hbm,
    rate_ref,
    gain_ref,
    out_ref,
    q_buf,
    k_buf,
    v_buf,
    att,
    first_term,
    s_own,
    s_in,
    t_own,
    t_in,
    total,
    f_in,
    b_in,
    pz_out,
    pz_in,
    px_out,
    before,
    sq_own,
    sq_in,
    load_sem,
    s_sem,
    t_sem,
    f_sem,
    b_sem,
    pz_sem,
    px_sem,
    sq_sem,
):
    nz, nx, nt = sizes
    groups = nz // GROUP
    forward, backward = groups // 2, groups - 1 - groups // 2
    rows = q_hbm.shape[0]
    blocks = rows // BLK
    span = rows
    slab = HEAD_DIM // GROUP
    f32, bf16 = jnp.float32, jnp.bfloat16

    z, x, t = lax.axis_index("ctx"), lax.axis_index("exp"), lax.axis_index("tp")
    low = lax.rem(z, GROUP)
    high = lax.div(z, GROUP)

    def x_at(k):
        return lax.rem(x + (k + nx), nx)

    def low_at(k):
        return lax.rem(low + (k + GROUP), GROUP)

    def z_at(k):
        return z - low + low_at(k)

    def t_at(k):
        return lax.rem(t + k, nt)

    z_up, z_down = lax.rem(z + GROUP, nz), lax.rem(z + nz - GROUP, nz)

    barrier = pltpu.get_barrier_semaphore()
    for k in range(1, GROUP):
        pl.semaphore_signal(barrier, inc=1, device_id={"ctx": z_at(k)}, device_id_type=MESH)
    pl.semaphore_signal(barrier, inc=1, device_id={"ctx": z_up}, device_id_type=MESH)
    pl.semaphore_signal(barrier, inc=1, device_id={"ctx": z_down}, device_id_type=MESH)
    for k in range(1, nx):
        pl.semaphore_signal(barrier, inc=1, device_id={"exp": x_at(k)}, device_id_type=MESH)
    for k in range(1, nt):
        pl.semaphore_signal(barrier, inc=1, device_id={"tp": t_at(k)}, device_id_type=MESH)

    def load(which, slot):
        source, target = ((k_hbm, k_buf), (v_hbm, v_buf), (q_hbm, q_buf))[which]
        lanes = pl.ds(pl.multiple_of(x_at(slot) * HEAD_DIM, HEAD_DIM), HEAD_DIM)
        return pltpu.make_async_copy(
            source.at[:, lanes], target.at[slot], load_sem.at[which, slot]
        )

    order = [2, 1, 3, 0] if nx == 4 else list(range(1, nx)) + [0]
    for slot in order:
        load(0, slot).start()
        load(1, slot).start()
    for slot in range(nx):
        load(2, slot).start()

    def rate_of(slot):
        return rate_ref[x_at(slot)]

    def decay(rate, distance, valid=None):
        distance = jnp.maximum(distance, 0)
        weight = jnp.exp(jnp.full((1, HEAD_DIM), -rate * distance.astype(f32), f32))
        if valid is not None:
            weight = weight * jnp.where(valid, 1.0, 0.0).astype(f32)
        return weight

    def fixed_decay(rate, distance):
        return jnp.exp(jnp.full((1, HEAD_DIM), -rate * float(distance), f32))

    def send_s(k):
        return pltpu.make_async_remote_copy(
            s_own.at[k], s_in.at[k - 1], s_sem.at[0, k - 1], s_sem.at[1, k - 1],
            device_id={"exp": x_at(k)}, device_id_type=MESH,
        )

    def send_t(k):
        return pltpu.make_async_remote_copy(
            t_own.at[low_at(k)], t_in.at[k - 1], t_sem.at[0, k - 1], t_sem.at[1, k - 1],
            device_id={"ctx": z_at(k)}, device_id_type=MESH,
        )

    def send_f(s):
        return pltpu.make_async_remote_copy(
            total if s == 0 else f_in.at[s - 1], f_in.at[s], f_sem.at[0, s], f_sem.at[1, s],
            device_id={"ctx": z_up}, device_id_type=MESH,
        )

    def send_b(s):
        return pltpu.make_async_remote_copy(
            total if s == 0 else b_in.at[s - 1], b_in.at[s], b_sem.at[0, s], b_sem.at[1, s],
            device_id={"ctx": z_down}, device_id_type=MESH,
        )

    def send_pz(k):
        return pltpu.make_async_remote_copy(
            pz_out.at[k], pz_in.at[k - 1], pz_sem.at[0, k - 1], pz_sem.at[1, k - 1],
            device_id={"ctx": z_at(k)}, device_id_type=MESH,
        )

    def send_px(q, k):
        return pltpu.make_async_remote_copy(
            px_out.at[q - 1, k], before.at[nx - q, low_at(-k)],
            px_sem.at[0, q - 1, k], px_sem.at[1, q - 1, k],
            device_id={"exp": x_at(q)}, device_id_type=MESH,
        )

    def send_sq(k):
        return pltpu.make_async_remote_copy(
            sq_own, sq_in.at[k - 1], sq_sem.at[0, k - 1], sq_sem.at[1, k - 1],
            device_id={"tp": t_at(k)}, device_id_type=MESH,
        )

    position = lax.broadcasted_iota(jnp.int32, (BLK, HEAD_DIM), 0).astype(f32)
    entered = False
    for slot in order:
        rate = rate_of(slot)
        load(0, slot).wait()
        load(1, slot).wait()
        tail = jnp.exp(-rate * (BLK - position))
        block_decay = fixed_decay(rate, BLK)
        state = None
        for block in range(blocks):
            at = pl.ds(block * BLK, BLK)
            scaled = (k_buf[slot, at, :].astype(f32) * tail).astype(bf16)
            term = lax.dot_general(
                scaled, v_buf[slot, at, :], (((0,), (0,)), ((), ())), preferred_element_type=f32
            )
            if block < blocks - 1:
                first_term[slot, block] = term
            state = term if state is None else block_decay * state + term
        s_own[slot] = state
        if not entered:
            pl.semaphore_wait(barrier, (GROUP - 1) + 2 + (nx - 1) + (nt - 1))
            entered = True
        if slot != 0:
            send_s(slot).start()

    rate = rate_of(0)
    x_weight = [decay(rate, span * (nx - 1 - x_at(-k))) for k in range(nx)]
    plane = x_weight[0] * s_own[0]
    for k in range(1, nx):
        send_s(k).wait_recv()
        plane = plane + x_weight[k] * s_in[k - 1]
    for i in range(GROUP):
        t_own[i] = plane[i * slab : (i + 1) * slab]
    for k in (3, 2, 1):
        send_t(k).start()
    z_span = span * nx
    z_weight = [decay(rate, z_span * (GROUP - 1 - low_at(-k))) for k in range(GROUP)]
    whole = z_weight[0] * t_own[low]
    for k in range(1, GROUP):
        send_t(k).wait_recv()
        whole = whole + z_weight[k] * t_in[k - 1]
    total[...] = whole
    send_f(0).start()
    if backward:
        send_b(0).start()

    line = lax.broadcasted_iota(jnp.int32, (BLK, BLK), 0)
    column = lax.broadcasted_iota(jnp.int32, (BLK, BLK), 1)
    causal = line >= column
    spread = jnp.maximum(line - column, 0).astype(f32)

    def mix(slot):
        load(2, slot).wait()
        weight = jnp.where(causal, jnp.exp(-rate_of(slot) * spread), 0.0)
        for block in range(blocks):
            at = pl.ds(block * BLK, BLK)
            scores = lax.dot_general(
                q_buf[slot, at, :], k_buf[slot, at, :], (((1,), (1,)), ((), ())),
                preferred_element_type=f32,
            )
            mixing = (scores * weight).astype(bf16)
            att[slot, at, :] = jnp.dot(mixing, v_buf[slot, at, :], preferred_element_type=f32)

    group_span = z_span * GROUP
    pending = list(range(nx))
    for s in range(forward):
        take = -(-len(pending) // (forward - s))
        for slot in pending[:take]:
            mix(slot)
        pending = pending[take:]
        send_f(s).wait_recv()
        if s + 1 < forward:
            send_f(s + 1).start()
        if s < backward:
            send_b(s).wait_recv()
            if s + 1 < backward:
                send_b(s + 1).start()

    incoming = jnp.zeros((slab, HEAD_DIM), f32)
    for s in range(forward):
        incoming = incoming + decay(rate, jnp.int32(group_span * s), high - (s + 1) >= 0) * f_in[s]
    for s in range(backward):
        far = jnp.int32(group_span * (groups - 2 - s))
        incoming = incoming + decay(rate, far, high + (s + 1) - groups >= 0) * b_in[s]

    slabs = [t_own[low]] + [t_in[k - 1] for k in range(1, GROUP)]
    for k in (3, 2, 1, 0):
        goal = low_at(k)
        value = decay(rate, z_span * goal) * incoming
        for j in range(GROUP):
            source = low_at(-j)
            value = value + decay(rate, z_span * (goal - 1 - source), source < goal) * slabs[j]
        pz_out[k] = value
        if k:
            send_pz(k).start()

    weights = []
    for q in range(nx):
        goal = x_at(q)
        weights.append(
            (
                decay(rate, span * goal),
                [
                    decay(rate, span * (goal - 1 - x_at(-j)), x_at(-j) < goal)
                    for j in range(nx)
                ],
            )
        )
    for k in range(GROUP):
        if k:
            send_pz(k).wait_recv()
            base = pz_in[k - 1]
        else:
            base = pz_out[0]
        index = low_at(-k)
        at = pl.ds(pl.multiple_of(index * slab, slab), slab)
        terms = [s_own[0, at, :]] + [s_in[j - 1, at, :] for j in range(1, nx)]
        for q in (2, 1, 3, 0) if nx == 4 else tuple(range(1, nx)) + (0,):
            entry, inner = weights[q]
            value = entry * base
            for j in range(nx):
                value = value + inner[j] * terms[j]
            if q:
                px_out[q - 1, k] = value
                send_px(q, k).start()
            else:
                before[0, index] = value

    squares = [jnp.zeros((BLK, HEAD_DIM), f32) for block in range(blocks)]
    for q in range(nx):
        slot = (nx - q) % nx
        if q:
            for k in range(GROUP):
                pltpu.make_async_remote_copy(
                    px_out.at[q - 1, k], before.at[slot, low_at(-k)],
                    px_sem.at[0, q - 1, k], px_sem.at[1, q - 1, k],
                    device_id={"exp": x_at(q)}, device_id_type=MESH,
                ).wait_recv()
        rate = rate_of(slot)
        inner_decay = jnp.exp(-rate * position)
        block_decay = fixed_decay(rate, BLK)
        state = before[slot].reshape(HEAD_DIM, HEAD_DIM)
        for block in range(blocks):
            at = pl.ds(block * BLK, BLK)
            carried = jnp.dot(
                q_buf[slot, at, :], state.astype(bf16), preferred_element_type=f32
            )
            attended = att[slot, at, :] + carried * inner_decay
            att[slot, at, :] = attended
            squares[block] = squares[block] + attended * attended
            if block < blocks - 1:
                state = block_decay * state + first_term[slot, block]

    pieces = rows // HEAD_DIM
    per_block = BLK // HEAD_DIM
    for c in range(pieces):
        part = squares[c // per_block][(c % per_block) * HEAD_DIM : (c % per_block + 1) * HEAD_DIM]
        sq_own[pl.ds(c, 1), :] = jnp.sum(part.T, axis=0, keepdims=True)
    for k in range(1, nt):
        send_sq(k).start()
    sum_squares = sq_own[...]
    for k in range(1, nt):
        send_sq(k).wait_recv()
        sum_squares = sum_squares + sq_in[k - 1]
    scale = lax.rsqrt(sum_squares / (nt * nx * HEAD_DIM) + 1e-06)
    for c in range(pieces):
        at = pl.ds(c * HEAD_DIM, HEAD_DIM)
        row_scale = jnp.broadcast_to(scale[c : c + 1], (HEAD_DIM, HEAD_DIM)).T
        for slot in range(nx):
            head = x_at(slot)
            lanes = pl.ds(pl.multiple_of(head * HEAD_DIM, HEAD_DIM), HEAD_DIM)
            gain = gain_ref[pl.ds(head, 1), :]
            out_ref[at, lanes] = (att[slot, at, :] * row_scale * gain).astype(bf16)

    for k in range(1, nx):
        send_s(k).wait_send()
        for c in range(GROUP):
            send_px(k, c).wait_send()
    for k in range(1, GROUP):
        send_t(k).wait_send()
        send_pz(k).wait_send()
    for s in range(forward):
        send_f(s).wait_send()
    for s in range(backward):
        send_b(s).wait_send()
    for k in range(1, nt):
        send_sq(k).wait_send()


def solution(mesh):
    nz, nx, nt = mesh.shape["ctx"], mesh.shape["exp"], mesh.shape["tp"]
    groups = nz // GROUP
    forward, backward = groups // 2, groups - 1 - groups // 2
    slab = HEAD_DIM // GROUP

    def local(queries, key_vectors, value_vectors, decay_rate, norm_gain):
        rows, width = queries.shape
        heads = width // HEAD_DIM
        blocks = rows // BLK
        f32 = jnp.float32
        square = (HEAD_DIM, HEAD_DIM)
        piece = (slab, HEAD_DIM)
        dma = pltpu.SemaphoreType.DMA
        scratch = [
            pltpu.VMEM((heads, rows, HEAD_DIM), jnp.bfloat16),
            pltpu.VMEM((heads, rows, HEAD_DIM), jnp.bfloat16),
            pltpu.VMEM((heads, rows, HEAD_DIM), jnp.bfloat16),
            pltpu.VMEM((heads, rows, HEAD_DIM), f32),
            pltpu.VMEM((heads, max(blocks - 1, 1)) + square, f32),
            pltpu.VMEM((heads,) + square, f32),
            pltpu.VMEM((nx - 1,) + square, f32),
            pltpu.VMEM((GROUP,) + piece, f32),
            pltpu.VMEM((GROUP - 1,) + piece, f32),
            pltpu.VMEM(piece, f32),
            pltpu.VMEM((forward,) + piece, f32),
            pltpu.VMEM((max(backward, 1),) + piece, f32),
            pltpu.VMEM((GROUP,) + piece, f32),
            pltpu.VMEM((GROUP - 1,) + piece, f32),
            pltpu.VMEM((nx - 1, GROUP) + piece, f32),
            pltpu.VMEM((heads, GROUP) + piece, f32),
            pltpu.VMEM((rows // HEAD_DIM, HEAD_DIM), f32),
            pltpu.VMEM((nt - 1, rows // HEAD_DIM, HEAD_DIM), f32),
            dma((3, heads)),
            dma((2, nx - 1)),
            dma((2, GROUP - 1)),
            dma((2, forward)),
            dma((2, max(backward, 1))),
            dma((2, GROUP - 1)),
            dma((2, nx - 1, GROUP)),
            dma((2, nt - 1)),
        ]
        return pl.pallas_call(
            functools.partial(kernel, (nz, nx, nt)),
            out_shape=jax.ShapeDtypeStruct((rows, width), jnp.bfloat16),
            in_specs=[
                pl.BlockSpec(memory_space=pl.ANY),
                pl.BlockSpec(memory_space=pl.ANY),
                pl.BlockSpec(memory_space=pl.ANY),
                pl.BlockSpec(memory_space=pltpu.SMEM),
                pl.BlockSpec(memory_space=pltpu.VMEM),
            ],
            out_specs=pl.BlockSpec(memory_space=pltpu.VMEM),
            scratch_shapes=scratch,
            compiler_params=pltpu.CompilerParams(collective_id=0, has_side_effects=True),
            name="lightning",
        )(queries, key_vectors, value_vectors, decay_rate, norm_gain.reshape(heads, HEAD_DIM))

    return jax.shard_map(
        local,
        mesh=mesh,
        in_specs=(
            P(("ctx", "exp"), "tp"),
            P(("ctx", "exp"), "tp"),
            P(("ctx", "exp"), "tp"),
            P("tp"),
            P("tp"),
        ),
        out_specs=P(("ctx", "exp"), "tp"),
        check_vma=False,
    )
```

```python
import functools

import jax
import jax.numpy as jnp
from jax import lax
from jax.experimental import pallas as pl
from jax.experimental.pallas import tpu as pltpu
from jax.sharding import PartitionSpec as P

HEADS = 32
HEAD_DIM = 128
BLK = 256
GROUP = 4
MESH = pl.DeviceIdType.MESH


def kernel(
    sizes,
    q_hbm,
    k_hbm,
    v_hbm,
    rate_ref,
    gain_ref,
    out_ref,
    q_buf,
    k_buf,
    v_buf,
    att,
    first_term,
    s_own,
    s_in,
    t_own,
    t_in,
    up_out,
    up_in,
    pz_out,
    pz_in,
    px_out,
    before,
    sq_own,
    sq_in,
    load_sem,
    s_sem,
    t_sem,
    up_sem,
    pz_sem,
    px_sem,
    sq_sem,
):
    nz, nx, nt = sizes
    groups = nz // GROUP
    rows = q_hbm.shape[0]
    blocks = rows // BLK
    span = rows
    slab = HEAD_DIM // GROUP
    f32, bf16 = jnp.float32, jnp.bfloat16

    z, x, t = lax.axis_index("ctx"), lax.axis_index("exp"), lax.axis_index("tp")
    low = lax.rem(z, GROUP)
    high = lax.div(z, GROUP)

    def x_at(k):
        return lax.rem(x + (k + nx), nx)

    def low_at(k):
        return lax.rem(low + (k + GROUP), GROUP)

    def z_at(k):
        return z - low + low_at(k)

    def t_at(k):
        return lax.rem(t + k, nt)

    z_up, z_down = lax.rem(z + GROUP, nz), lax.rem(z + nz - GROUP, nz)
    has_up = high < groups - 1

    barrier = pltpu.get_barrier_semaphore()
    for k in range(1, GROUP):
        pl.semaphore_signal(barrier, inc=1, device_id={"ctx": z_at(k)}, device_id_type=MESH)

    @pl.when(high > 0)
    def _():
        pl.semaphore_signal(barrier, inc=1, device_id={"ctx": z_down}, device_id_type=MESH)

    for k in range(1, nx):
        pl.semaphore_signal(barrier, inc=1, device_id={"exp": x_at(k)}, device_id_type=MESH)
    for k in range(1, nt):
        pl.semaphore_signal(barrier, inc=1, device_id={"tp": t_at(k)}, device_id_type=MESH)

    def load(which, slot):
        source, target = ((k_hbm, k_buf), (v_hbm, v_buf), (q_hbm, q_buf))[which]
        lanes = pl.ds(pl.multiple_of(x_at(slot) * HEAD_DIM, HEAD_DIM), HEAD_DIM)
        return pltpu.make_async_copy(
            source.at[:, lanes], target.at[slot], load_sem.at[which, slot]
        )

    order = [2, 1, 3, 0] if nx == 4 else list(range(1, nx)) + [0]
    for slot in order:
        load(0, slot).start()
        load(1, slot).start()
    for slot in range(nx):
        load(2, slot).start()

    def rate_of(slot):
        return rate_ref[x_at(slot)]

    def decay(rate, distance, valid=None):
        distance = jnp.maximum(distance, 0)
        weight = jnp.exp(jnp.full((1, HEAD_DIM), -rate * distance.astype(f32), f32))
        if valid is not None:
            weight = weight * jnp.where(valid, 1.0, 0.0).astype(f32)
        return weight

    def fixed_decay(rate, distance):
        return jnp.exp(jnp.full((1, HEAD_DIM), -rate * float(distance), f32))

    def send_s(k, o):
        return pltpu.make_async_remote_copy(
            s_own.at[k, low_at(o)], s_in.at[k - 1, low_at(o)],
            s_sem.at[0, k - 1, o], s_sem.at[1, k - 1, o],
            device_id={"exp": x_at(k)}, device_id_type=MESH,
        )

    def send_t(k):
        return pltpu.make_async_remote_copy(
            t_own.at[k], t_in.at[k - 1], t_sem.at[0, k - 1], t_sem.at[1, k - 1],
            device_id={"ctx": z_at(k)}, device_id_type=MESH,
        )

    def send_up():
        return pltpu.make_async_remote_copy(
            up_out, up_in, up_sem.at[0], up_sem.at[1],
            device_id={"ctx": z_up}, device_id_type=MESH,
        )

    def send_pz(k):
        return pltpu.make_async_remote_copy(
            pz_out.at[k], pz_in.at[k - 1], pz_sem.at[0, k - 1], pz_sem.at[1, k - 1],
            device_id={"ctx": z_at(k)}, device_id_type=MESH,
        )

    def send_px(q, k):
        return pltpu.make_async_remote_copy(
            px_out.at[q - 1, k], before.at[nx - q, low_at(-k)],
            px_sem.at[0, q - 1, k], px_sem.at[1, q - 1, k],
            device_id={"exp": x_at(q)}, device_id_type=MESH,
        )

    def send_sq(k):
        return pltpu.make_async_remote_copy(
            sq_own, sq_in.at[k - 1], sq_sem.at[0, k - 1], sq_sem.at[1, k - 1],
            device_id={"tp": t_at(k)}, device_id_type=MESH,
        )

    position = lax.broadcasted_iota(jnp.int32, (BLK, HEAD_DIM), 0).astype(f32)
    entered = False
    for slot in order:
        rate = rate_of(slot)
        load(0, slot).wait()
        load(1, slot).wait()
        tail = jnp.exp(-rate * (BLK - position))
        block_decay = fixed_decay(rate, BLK)
        state = None
        for block in range(blocks):
            at = pl.ds(block * BLK, BLK)
            scaled = (k_buf[slot, at, :].astype(f32) * tail).astype(bf16)
            term = lax.dot_general(
                scaled, v_buf[slot, at, :], (((0,), (0,)), ((), ())), preferred_element_type=f32
            )
            if block < blocks - 1:
                first_term[slot, block] = term
            state = term if state is None else block_decay * state + term
        s_own[slot] = state.reshape(GROUP, slab, HEAD_DIM)
        if not entered:
            partners = (GROUP - 1) + (nx - 1) + (nt - 1)

            @pl.when(has_up)
            def _():
                pl.semaphore_wait(barrier, partners + 1)

            @pl.when(jnp.logical_not(has_up))
            def _():
                pl.semaphore_wait(barrier, partners)

            entered = True
        if slot != 0:
            for o in (3, 2, 1, 0):
                send_s(slot, o).start()

    line = lax.broadcasted_iota(jnp.int32, (BLK, BLK), 0)
    column = lax.broadcasted_iota(jnp.int32, (BLK, BLK), 1)
    causal = line >= column
    spread = jnp.maximum(line - column, 0).astype(f32)
    for slot in range(nx):
        load(2, slot).wait()
        weight = jnp.where(causal, jnp.exp(-rate_of(slot) * spread), 0.0)
        for block in range(blocks):
            at = pl.ds(block * BLK, BLK)
            scores = lax.dot_general(
                q_buf[slot, at, :], k_buf[slot, at, :], (((1,), (1,)), ((), ())),
                preferred_element_type=f32,
            )
            mixing = (scores * weight).astype(bf16)
            att[slot, at, :] = jnp.dot(mixing, v_buf[slot, at, :], preferred_element_type=f32)

    rate = rate_of(0)
    x_weight = [decay(rate, span * (nx - 1 - x_at(-k))) for k in range(nx)]
    z_span = span * nx
    z_weight = [decay(rate, z_span * (GROUP - 1 - low_at(-k))) for k in range(GROUP)]
    for o in (3, 2, 1, 0):
        plane = x_weight[0] * s_own[0, low_at(o)]
        for k in range(1, nx):
            send_s(k, o).wait_recv()
            plane = plane + x_weight[k] * s_in[k - 1, low_at(o)]
        t_own[o] = plane
        if o:
            send_t(o).start()
    whole = z_weight[0] * t_own[0]
    for k in range(1, GROUP):
        send_t(k).wait_recv()
        whole = whole + z_weight[k] * t_in[k - 1]

    @pl.when(high > 0)
    def _():
        send_up().wait_recv()

    @pl.when(high == 0)
    def _():
        up_in[...] = jnp.zeros_like(up_in)

    incoming = up_in[...]

    @pl.when(has_up)
    def _():
        up_out[...] = whole + fixed_decay(rate, z_span * GROUP) * incoming
        send_up().start()

    slabs = [t_own[0]] + [t_in[k - 1] for k in range(1, GROUP)]
    for k in (3, 2, 1, 0):
        goal = low_at(k)
        value = decay(rate, z_span * goal) * incoming
        for j in range(GROUP):
            source = low_at(-j)
            value = value + decay(rate, z_span * (goal - 1 - source), source < goal) * slabs[j]
        pz_out[k] = value
        if k:
            send_pz(k).start()

    weights = []
    for q in range(nx):
        goal = x_at(q)
        weights.append(
            (
                decay(rate, span * goal),
                [
                    decay(rate, span * (goal - 1 - x_at(-j)), x_at(-j) < goal)
                    for j in range(nx)
                ],
            )
        )
    for k in range(GROUP):
        if k:
            send_pz(k).wait_recv()
            base = pz_in[k - 1]
        else:
            base = pz_out[0]
        index = low_at(-k)
        terms = [s_own[0, index]] + [s_in[j - 1, index] for j in range(1, nx)]
        for q in (2, 1, 3, 0) if nx == 4 else tuple(range(1, nx)) + (0,):
            entry, inner = weights[q]
            value = entry * base
            for j in range(nx):
                value = value + inner[j] * terms[j]
            if q:
                px_out[q - 1, k] = value
                send_px(q, k).start()
            else:
                before[0, index] = value

    squares = [jnp.zeros((BLK, HEAD_DIM), f32) for block in range(blocks)]
    for q in range(nx):
        slot = (nx - q) % nx
        if q:
            for k in range(GROUP):
                pltpu.make_async_remote_copy(
                    px_out.at[q - 1, k], before.at[slot, low_at(-k)],
                    px_sem.at[0, q - 1, k], px_sem.at[1, q - 1, k],
                    device_id={"exp": x_at(q)}, device_id_type=MESH,
                ).wait_recv()
        rate = rate_of(slot)
        inner_decay = jnp.exp(-rate * position)
        block_decay = fixed_decay(rate, BLK)
        state = before[slot].reshape(HEAD_DIM, HEAD_DIM)
        for block in range(blocks):
            at = pl.ds(block * BLK, BLK)
            carried = jnp.dot(
                q_buf[slot, at, :], state.astype(bf16), preferred_element_type=f32
            )
            attended = att[slot, at, :] + carried * inner_decay
            att[slot, at, :] = attended
            squares[block] = squares[block] + attended * attended
            if block < blocks - 1:
                state = block_decay * state + first_term[slot, block]

    pieces = rows // HEAD_DIM
    per_block = BLK // HEAD_DIM
    for c in range(pieces):
        part = squares[c // per_block][(c % per_block) * HEAD_DIM : (c % per_block + 1) * HEAD_DIM]
        sq_own[pl.ds(c, 1), :] = jnp.sum(part.T, axis=0, keepdims=True)
    for k in range(1, nt):
        send_sq(k).start()
    sum_squares = sq_own[...]
    for k in range(1, nt):
        send_sq(k).wait_recv()
        sum_squares = sum_squares + sq_in[k - 1]
    scale = lax.rsqrt(sum_squares / (nt * nx * HEAD_DIM) + 1e-06)
    for c in range(pieces):
        at = pl.ds(c * HEAD_DIM, HEAD_DIM)
        row_scale = jnp.broadcast_to(scale[c : c + 1], (HEAD_DIM, HEAD_DIM)).T
        for slot in range(nx):
            head = x_at(slot)
            lanes = pl.ds(pl.multiple_of(head * HEAD_DIM, HEAD_DIM), HEAD_DIM)
            gain = gain_ref[pl.ds(head, 1), :]
            out_ref[at, lanes] = (att[slot, at, :] * row_scale * gain).astype(bf16)

    for k in range(1, nx):
        for c in range(GROUP):
            send_s(k, c).wait_send()
            send_px(k, c).wait_send()
    for k in range(1, GROUP):
        send_t(k).wait_send()
        send_pz(k).wait_send()

    @pl.when(has_up)
    def _():
        send_up().wait_send()

    for k in range(1, nt):
        send_sq(k).wait_send()


def solution(mesh):
    nz, nx, nt = mesh.shape["ctx"], mesh.shape["exp"], mesh.shape["tp"]
    slab = HEAD_DIM // GROUP

    def local(queries, key_vectors, value_vectors, decay_rate, norm_gain):
        rows, width = queries.shape
        heads = width // HEAD_DIM
        blocks = rows // BLK
        f32 = jnp.float32
        square = (HEAD_DIM, HEAD_DIM)
        piece = (slab, HEAD_DIM)
        dma = pltpu.SemaphoreType.DMA
        scratch = [
            pltpu.VMEM((heads, rows, HEAD_DIM), jnp.bfloat16),
            pltpu.VMEM((heads, rows, HEAD_DIM), jnp.bfloat16),
            pltpu.VMEM((heads, rows, HEAD_DIM), jnp.bfloat16),
            pltpu.VMEM((heads, rows, HEAD_DIM), f32),
            pltpu.VMEM((heads, max(blocks - 1, 1)) + square, f32),
            pltpu.VMEM((heads, GROUP) + piece, f32),
            pltpu.VMEM((nx - 1, GROUP) + piece, f32),
            pltpu.VMEM((GROUP,) + piece, f32),
            pltpu.VMEM((GROUP - 1,) + piece, f32),
            pltpu.VMEM(piece, f32),
            pltpu.VMEM(piece, f32),
            pltpu.VMEM((GROUP,) + piece, f32),
            pltpu.VMEM((GROUP - 1,) + piece, f32),
            pltpu.VMEM((nx - 1, GROUP) + piece, f32),
            pltpu.VMEM((heads, GROUP) + piece, f32),
            pltpu.VMEM((rows // HEAD_DIM, HEAD_DIM), f32),
            pltpu.VMEM((nt - 1, rows // HEAD_DIM, HEAD_DIM), f32),
            dma((3, heads)),
            dma((2, nx - 1, GROUP)),
            dma((2, GROUP - 1)),
            dma((2,)),
            dma((2, GROUP - 1)),
            dma((2, nx - 1, GROUP)),
            dma((2, nt - 1)),
        ]
        return pl.pallas_call(
            functools.partial(kernel, (nz, nx, nt)),
            out_shape=jax.ShapeDtypeStruct((rows, width), jnp.bfloat16),
            in_specs=[
                pl.BlockSpec(memory_space=pl.ANY),
                pl.BlockSpec(memory_space=pl.ANY),
                pl.BlockSpec(memory_space=pl.ANY),
                pl.BlockSpec(memory_space=pltpu.SMEM),
                pl.BlockSpec(memory_space=pltpu.VMEM),
            ],
            out_specs=pl.BlockSpec(memory_space=pltpu.VMEM),
            scratch_shapes=scratch,
            compiler_params=pltpu.CompilerParams(collective_id=0, has_side_effects=True),
            name="lightning",
        )(queries, key_vectors, value_vectors, decay_rate, norm_gain.reshape(heads, HEAD_DIM))

    return jax.shard_map(
        local,
        mesh=mesh,
        in_specs=(
            P(("ctx", "exp"), "tp"),
            P(("ctx", "exp"), "tp"),
            P(("ctx", "exp"), "tp"),
            P("tp"),
            P("tp"),
        ),
        out_specs=P(("ctx", "exp"), "tp"),
        check_vma=False,
    )
```

```python
import functools

import jax
import jax.numpy as jnp
from jax import lax
from jax.experimental import pallas as pl
from jax.experimental.pallas import tpu as pltpu
from jax.sharding import PartitionSpec as P

HEADS = 32
HEAD_DIM = 128
BLK = 256
GROUP = 4
MESH = pl.DeviceIdType.MESH


def kernel(
    sizes,
    q_hbm,
    k_hbm,
    v_hbm,
    rate_hbm,
    gain_hbm,
    out_ref,
    rate_ref,
    gain_ref,
    q_buf,
    k_buf,
    v_buf,
    att,
    first_term,
    s_own,
    s_in,
    t_own,
    t_in,
    up_out,
    up_in,
    pz_out,
    pz_in,
    px_out,
    before,
    sq_own,
    sq_in,
    load_sem,
    rate_sem,
    gain_sem,
    below_sem,
    above_sem,
    s_sem,
    t_sem,
    up_sem,
    pz_sem,
    px_sem,
    sq_sem,
):
    nz, nx, nt = sizes
    groups = nz // GROUP
    rows = q_hbm.shape[0]
    blocks = rows // BLK
    span = rows
    slab = HEAD_DIM // GROUP
    f32, bf16 = jnp.float32, jnp.bfloat16

    z, x, t = lax.axis_index("ctx"), lax.axis_index("exp"), lax.axis_index("tp")
    low = lax.rem(z, GROUP)
    high = lax.div(z, GROUP)

    def x_at(k):
        return lax.rem(x + (k + nx), nx)

    def low_at(k):
        return lax.rem(low + (k + GROUP), GROUP)

    def z_at(k):
        return z - low + low_at(k)

    def t_at(k):
        return lax.rem(t + k, nt)

    z_up, z_down = lax.rem(z + GROUP, nz), lax.rem(z + nz - GROUP, nz)
    has_up = high < groups - 1

    barrier = pltpu.get_barrier_semaphore()
    for k in range(1, GROUP):
        pl.semaphore_signal(barrier, inc=1, device_id={"ctx": z_at(k)}, device_id_type=MESH)

    top = jnp.logical_and(low == GROUP - 1, has_up)
    bottom = jnp.logical_and(low == 0, high > 0)

    @pl.when(top)
    def _():
        pl.semaphore_signal(barrier, inc=1, device_id={"ctx": z + 1}, device_id_type=MESH)

    @pl.when(bottom)
    def _():
        pl.semaphore_signal(barrier, inc=1, device_id={"ctx": z - 1}, device_id_type=MESH)

    for k in range(1, nx):
        pl.semaphore_signal(barrier, inc=1, device_id={"exp": x_at(k)}, device_id_type=MESH)
    for k in range(1, nt):
        pl.semaphore_signal(barrier, inc=1, device_id={"tp": t_at(k)}, device_id_type=MESH)

    def load(which, slot):
        source, target = ((k_hbm, k_buf), (v_hbm, v_buf), (q_hbm, q_buf))[which]
        lanes = pl.ds(pl.multiple_of(x_at(slot) * HEAD_DIM, HEAD_DIM), HEAD_DIM)
        return pltpu.make_async_copy(
            source.at[:, lanes], target.at[slot], load_sem.at[which, slot]
        )

    rate_copy = pltpu.make_async_copy(rate_hbm, rate_ref, rate_sem)
    gain_copy = pltpu.make_async_copy(gain_hbm, gain_ref, gain_sem)
    rate_copy.start()
    order = [2, 1, 3, 0] if nx == 4 else list(range(1, nx)) + [0]
    for slot in order:
        load(0, slot).start()
        load(1, slot).start()
    for slot in range(nx):
        load(2, slot).start()
    gain_copy.start()

    def rate_of(slot):
        return rate_ref[x_at(slot)]

    def decay(rate, distance, valid=None):
        distance = jnp.maximum(distance, 0)
        weight = jnp.exp(jnp.full((1, HEAD_DIM), -rate * distance.astype(f32), f32))
        if valid is not None:
            weight = weight * jnp.where(valid, 1.0, 0.0).astype(f32)
        return weight

    def fixed_decay(rate, distance):
        return jnp.exp(jnp.full((1, HEAD_DIM), -rate * float(distance), f32))

    def send_s(k, o):
        return pltpu.make_async_remote_copy(
            s_own.at[k, low_at(o)], s_in.at[k - 1, low_at(o)],
            s_sem.at[0, k - 1, o], s_sem.at[1, k - 1, o],
            device_id={"exp": x_at(k)}, device_id_type=MESH,
        )

    def send_t(k):
        return pltpu.make_async_remote_copy(
            t_own.at[k], t_in.at[k - 1], t_sem.at[0, k - 1], t_sem.at[1, k - 1],
            device_id={"ctx": z_at(k)}, device_id_type=MESH,
        )

    def send_up():
        return pltpu.make_async_remote_copy(
            up_out, up_in, up_sem.at[0], up_sem.at[1],
            device_id={"ctx": z_up}, device_id_type=MESH,
        )

    def send_pz(k):
        return pltpu.make_async_remote_copy(
            pz_out.at[k], pz_in.at[k - 1], pz_sem.at[0, k - 1], pz_sem.at[1, k - 1],
            device_id={"ctx": z_at(k)}, device_id_type=MESH,
        )

    def send_px(q, k):
        return pltpu.make_async_remote_copy(
            px_out.at[q - 1, k], before.at[nx - q, low_at(-k)],
            px_sem.at[0, q - 1, k], px_sem.at[1, q - 1, k],
            device_id={"exp": x_at(q)}, device_id_type=MESH,
        )

    def send_sq(k):
        return pltpu.make_async_remote_copy(
            sq_own, sq_in.at[k - 1], sq_sem.at[0, k - 1], sq_sem.at[1, k - 1],
            device_id={"tp": t_at(k)}, device_id_type=MESH,
        )

    position = lax.broadcasted_iota(jnp.int32, (BLK, HEAD_DIM), 0).astype(f32)
    entered = False
    rate_copy.wait()
    for slot in order:
        rate = rate_of(slot)
        load(0, slot).wait()
        load(1, slot).wait()
        tail = jnp.exp(-rate * (BLK - position))
        block_decay = fixed_decay(rate, BLK)
        state = None
        for block in range(blocks):
            at = pl.ds(block * BLK, BLK)
            scaled = (k_buf[slot, at, :].astype(f32) * tail).astype(bf16)
            term = lax.dot_general(
                scaled, v_buf[slot, at, :], (((0,), (0,)), ((), ())), preferred_element_type=f32
            )
            if block < blocks - 1:
                first_term[slot, block] = term
            state = term if state is None else block_decay * state + term
        s_own[slot] = state.reshape(GROUP, slab, HEAD_DIM)
        if not entered:
            partners = (GROUP - 1) + (nx - 1) + (nt - 1)

            edge = jnp.logical_or(top, bottom)

            @pl.when(edge)
            def _():
                pl.semaphore_wait(barrier, partners + 1)

            @pl.when(jnp.logical_not(edge))
            def _():
                pl.semaphore_wait(barrier, partners)

            entered = True
        if slot != 0:
            for o in (3, 2, 1, 0):
                send_s(slot, o).start()

    @pl.when(top)
    def _():
        pl.semaphore_signal(below_sem, inc=1, device_id={"ctx": z + 1}, device_id_type=MESH)

    line = lax.broadcasted_iota(jnp.int32, (BLK, BLK), 0)
    column = lax.broadcasted_iota(jnp.int32, (BLK, BLK), 1)
    causal = line >= column
    spread = jnp.maximum(line - column, 0).astype(f32)
    for slot in range(nx):
        load(2, slot).wait()
        weight = jnp.where(causal, jnp.exp(-rate_of(slot) * spread), 0.0)
        for block in range(blocks):
            at = pl.ds(block * BLK, BLK)
            scores = lax.dot_general(
                q_buf[slot, at, :], k_buf[slot, at, :], (((1,), (1,)), ((), ())),
                preferred_element_type=f32,
            )
            mixing = (scores * weight).astype(bf16)
            att[slot, at, :] = jnp.dot(mixing, v_buf[slot, at, :], preferred_element_type=f32)

    @pl.when(bottom)
    def _():
        pl.semaphore_wait(below_sem, 1)
        for k in range(1, GROUP + 1):
            pl.semaphore_signal(above_sem, inc=1, device_id={"ctx": z - k}, device_id_type=MESH)

    rate = rate_of(0)
    x_weight = [decay(rate, span * (nx - 1 - x_at(-k))) for k in range(nx)]
    z_span = span * nx
    z_weight = [decay(rate, z_span * (GROUP - 1 - low_at(-k))) for k in range(GROUP)]
    for o in (3, 2, 1, 0):
        plane = x_weight[0] * s_own[0, low_at(o)]
        for k in range(1, nx):
            send_s(k, o).wait_recv()
            plane = plane + x_weight[k] * s_in[k - 1, low_at(o)]
        t_own[o] = plane
        if o:
            send_t(o).start()
    whole = z_weight[0] * t_own[0]
    for k in range(1, GROUP):
        send_t(k).wait_recv()
        whole = whole + z_weight[k] * t_in[k - 1]

    @pl.when(high > 0)
    def _():
        send_up().wait_recv()

    @pl.when(high == 0)
    def _():
        up_in[...] = jnp.zeros_like(up_in)

    incoming = up_in[...]

    @pl.when(has_up)
    def _():
        pl.semaphore_wait(above_sem, 1)
        up_out[...] = whole + fixed_decay(rate, z_span * GROUP) * incoming
        send_up().start()

    slabs = [t_own[0]] + [t_in[k - 1] for k in range(1, GROUP)]
    for k in (3, 2, 1, 0):
        goal = low_at(k)
        value = decay(rate, z_span * goal) * incoming
        for j in range(GROUP):
            source = low_at(-j)
            value = value + decay(rate, z_span * (goal - 1 - source), source < goal) * slabs[j]
        pz_out[k] = value
        if k:
            send_pz(k).start()

    weights = []
    for q in range(nx):
        goal = x_at(q)
        weights.append(
            (
                decay(rate, span * goal),
                [
                    decay(rate, span * (goal - 1 - x_at(-j)), x_at(-j) < goal)
                    for j in range(nx)
                ],
            )
        )
    for k in range(GROUP):
        if k:
            send_pz(k).wait_recv()
            base = pz_in[k - 1]
        else:
            base = pz_out[0]
        index = low_at(-k)
        terms = [s_own[0, index]] + [s_in[j - 1, index] for j in range(1, nx)]
        for q in (2, 1, 3, 0) if nx == 4 else tuple(range(1, nx)) + (0,):
            entry, inner = weights[q]
            value = entry * base
            for j in range(nx):
                value = value + inner[j] * terms[j]
            if q:
                px_out[q - 1, k] = value
                send_px(q, k).start()
            else:
                before[0, index] = value

    squares = [jnp.zeros((BLK, HEAD_DIM), f32) for block in range(blocks)]
    for q in range(nx):
        slot = (nx - q) % nx
        if q:
            for k in range(GROUP):
                pltpu.make_async_remote_copy(
                    px_out.at[q - 1, k], before.at[slot, low_at(-k)],
                    px_sem.at[0, q - 1, k], px_sem.at[1, q - 1, k],
                    device_id={"exp": x_at(q)}, device_id_type=MESH,
                ).wait_recv()
        rate = rate_of(slot)
        inner_decay = jnp.exp(-rate * position)
        block_decay = fixed_decay(rate, BLK)
        state = before[slot].reshape(HEAD_DIM, HEAD_DIM)
        for block in range(blocks):
            at = pl.ds(block * BLK, BLK)
            carried = jnp.dot(
                q_buf[slot, at, :], state.astype(bf16), preferred_element_type=f32
            )
            attended = att[slot, at, :] + carried * inner_decay
            att[slot, at, :] = attended
            squares[block] = squares[block] + attended * attended
            if block < blocks - 1:
                state = block_decay * state + first_term[slot, block]

    pieces = rows // HEAD_DIM
    per_block = BLK // HEAD_DIM
    for c in range(pieces):
        part = squares[c // per_block][(c % per_block) * HEAD_DIM : (c % per_block + 1) * HEAD_DIM]
        sq_own[pl.ds(c, 1), :] = jnp.sum(part.T, axis=0, keepdims=True)
    for k in range(1, nt):
        send_sq(k).start()
    sum_squares = sq_own[...]
    for k in range(1, nt):
        send_sq(k).wait_recv()
        sum_squares = sum_squares + sq_in[k - 1]
    gain_copy.wait()
    scale = lax.rsqrt(sum_squares / (nt * nx * HEAD_DIM) + 1e-06)
    for c in range(pieces):
        at = pl.ds(c * HEAD_DIM, HEAD_DIM)
        row_scale = jnp.broadcast_to(scale[c : c + 1], (HEAD_DIM, HEAD_DIM)).T
        for slot in range(nx):
            head = x_at(slot)
            lanes = pl.ds(pl.multiple_of(head * HEAD_DIM, HEAD_DIM), HEAD_DIM)
            gain = gain_ref[pl.ds(head, 1), :]
            out_ref[at, lanes] = (att[slot, at, :] * row_scale * gain).astype(bf16)

    for k in range(1, nx):
        for c in range(GROUP):
            send_s(k, c).wait_send()
            send_px(k, c).wait_send()
    for k in range(1, GROUP):
        send_t(k).wait_send()
        send_pz(k).wait_send()

    @pl.when(has_up)
    def _():
        send_up().wait_send()

    for k in range(1, nt):
        send_sq(k).wait_send()


def solution(mesh):
    nz, nx, nt = mesh.shape["ctx"], mesh.shape["exp"], mesh.shape["tp"]
    slab = HEAD_DIM // GROUP

    def local(queries, key_vectors, value_vectors, decay_rate, norm_gain):
        rows, width = queries.shape
        heads = width // HEAD_DIM
        blocks = rows // BLK
        f32 = jnp.float32
        square = (HEAD_DIM, HEAD_DIM)
        piece = (slab, HEAD_DIM)
        dma = pltpu.SemaphoreType.DMA
        scratch = [
            pltpu.SMEM((heads,), f32),
            pltpu.VMEM((heads, HEAD_DIM), f32),
            pltpu.VMEM((heads, rows, HEAD_DIM), jnp.bfloat16),
            pltpu.VMEM((heads, rows, HEAD_DIM), jnp.bfloat16),
            pltpu.VMEM((heads, rows, HEAD_DIM), jnp.bfloat16),
            pltpu.VMEM((heads, rows, HEAD_DIM), f32),
            pltpu.VMEM((heads, max(blocks - 1, 1)) + square, f32),
            pltpu.VMEM((heads, GROUP) + piece, f32),
            pltpu.VMEM((nx - 1, GROUP) + piece, f32),
            pltpu.VMEM((GROUP,) + piece, f32),
            pltpu.VMEM((GROUP - 1,) + piece, f32),
            pltpu.VMEM(piece, f32),
            pltpu.VMEM(piece, f32),
            pltpu.VMEM((GROUP,) + piece, f32),
            pltpu.VMEM((GROUP - 1,) + piece, f32),
            pltpu.VMEM((nx - 1, GROUP) + piece, f32),
            pltpu.VMEM((heads, GROUP) + piece, f32),
            pltpu.VMEM((rows // HEAD_DIM, HEAD_DIM), f32),
            pltpu.VMEM((nt - 1, rows // HEAD_DIM, HEAD_DIM), f32),
            dma((3, heads)),
            dma,
            dma,
            pltpu.SemaphoreType.REGULAR,
            pltpu.SemaphoreType.REGULAR,
            dma((2, nx - 1, GROUP)),
            dma((2, GROUP - 1)),
            dma((2,)),
            dma((2, GROUP - 1)),
            dma((2, nx - 1, GROUP)),
            dma((2, nt - 1)),
        ]
        return pl.pallas_call(
            functools.partial(kernel, (nz, nx, nt)),
            out_shape=pltpu.VMEM((rows, width), jnp.bfloat16),
            in_specs=[
                pl.BlockSpec(memory_space=pl.ANY),
                pl.BlockSpec(memory_space=pl.ANY),
                pl.BlockSpec(memory_space=pl.ANY),
                pl.BlockSpec(memory_space=pl.ANY),
                pl.BlockSpec(memory_space=pl.ANY),
            ],
            out_specs=pl.BlockSpec(memory_space=pltpu.VMEM),
            scratch_shapes=scratch,
            compiler_params=pltpu.CompilerParams(collective_id=0, has_side_effects=True),
            name="lightning",
        )(queries, key_vectors, value_vectors, decay_rate, norm_gain.reshape(heads, HEAD_DIM))

    return jax.shard_map(
        local,
        mesh=mesh,
        in_specs=(
            P(("ctx", "exp"), "tp"),
            P(("ctx", "exp"), "tp"),
            P(("ctx", "exp"), "tp"),
            P("tp"),
            P("tp"),
        ),
        out_specs=P(("ctx", "exp"), "tp"),
        check_vma=False,
    )
```

```python
import functools

import jax
import jax.numpy as jnp
from jax import lax
from jax.experimental import pallas as pl
from jax.experimental.pallas import tpu as pltpu
from jax.sharding import PartitionSpec as P

HEADS = 32
HEAD_DIM = 128
BLK = 256
GROUP = 4
MESH = pl.DeviceIdType.MESH


def kernel(
    sizes,
    q_hbm,
    k_hbm,
    v_hbm,
    rate_hbm,
    gain_hbm,
    out_ref,
    rate_ref,
    gain_ref,
    q_buf,
    k_buf,
    v_buf,
    att,
    first_term,
    s_own,
    s_in,
    t_own,
    t_in,
    up_out,
    up_in,
    far_in,
    pz_out,
    pz_in,
    px_out,
    before,
    sq_own,
    sq_in,
    load_sem,
    rate_sem,
    gain_sem,
    up_ok,
    far_ok,
    s_sem,
    t_sem,
    up_sem,
    pz_sem,
    px_sem,
    sq_sem,
):
    nz, nx, nt = sizes
    groups = nz // GROUP
    rows = q_hbm.shape[0]
    blocks = rows // BLK
    span = rows
    slab = HEAD_DIM // GROUP
    f32, bf16 = jnp.float32, jnp.bfloat16

    z, x, t = lax.axis_index("ctx"), lax.axis_index("exp"), lax.axis_index("tp")
    low = lax.rem(z, GROUP)
    high = lax.div(z, GROUP)

    def x_at(k):
        return lax.rem(x + (k + nx), nx)

    def low_at(k):
        return lax.rem(low + (k + GROUP), GROUP)

    def z_at(k):
        return z - low + low_at(k)

    def t_at(k):
        return lax.rem(t + k, nt)

    half = groups // 2
    odd = lax.rem(high, 2) == 1
    has_down, has_up = high > 0, high < groups - 1
    takes_far = jnp.logical_and(odd, high >= half + 1)
    sends_far = jnp.logical_and(odd, jnp.logical_and(high >= half - 1, high < groups - 2))
    sends_total = jnp.logical_and(jnp.logical_not(odd), high >= half)

    def z_off(k):
        return lax.rem(z + (k + nz), nz)

    barrier = pltpu.get_barrier_semaphore()
    partners = (GROUP - 1) + (nx - 1) + (nt - 1)

    @pl.when(sends_far)
    def _():
        pl.semaphore_signal(
            barrier, inc=1, device_id={"ctx": z_off(2 * GROUP)}, device_id_type=MESH
        )

    @pl.when(has_up)
    def _():
        pl.semaphore_signal(barrier, inc=1, device_id={"ctx": z_off(GROUP)}, device_id_type=MESH)

    for k in range(1, GROUP):
        pl.semaphore_signal(barrier, inc=1, device_id={"ctx": z_at(k)}, device_id_type=MESH)
    for k in range(1, nx):
        pl.semaphore_signal(barrier, inc=1, device_id={"exp": x_at(k)}, device_id_type=MESH)
    for k in range(1, nt):
        pl.semaphore_signal(barrier, inc=1, device_id={"tp": t_at(k)}, device_id_type=MESH)

    def load(which, slot):
        source, target = ((k_hbm, k_buf), (v_hbm, v_buf), (q_hbm, q_buf))[which]
        lanes = pl.ds(pl.multiple_of(x_at(slot) * HEAD_DIM, HEAD_DIM), HEAD_DIM)
        return pltpu.make_async_copy(
            source.at[:, lanes], target.at[slot], load_sem.at[which, slot]
        )

    rate_copy = pltpu.make_async_copy(rate_hbm, rate_ref, rate_sem)
    gain_copy = pltpu.make_async_copy(gain_hbm, gain_ref, gain_sem)
    rate_copy.start()
    order = [2, 1, 3, 0] if nx == 4 else list(range(1, nx)) + [0]
    for slot in order:
        load(0, slot).start()
        load(1, slot).start()
    for slot in range(nx):
        load(2, slot).start()
    gain_copy.start()

    def rate_of(slot):
        return rate_ref[x_at(slot)]

    def decay(rate, distance, valid=None):
        distance = jnp.maximum(distance, 0)
        weight = jnp.exp(jnp.full((1, HEAD_DIM), -rate * distance.astype(f32), f32))
        if valid is not None:
            weight = weight * jnp.where(valid, 1.0, 0.0).astype(f32)
        return weight

    def fixed_decay(rate, distance):
        return jnp.exp(jnp.full((1, HEAD_DIM), -rate * float(distance), f32))

    def send_s(k, o):
        return pltpu.make_async_remote_copy(
            s_own.at[k, low_at(o)], s_in.at[k - 1, low_at(o)],
            s_sem.at[0, k - 1, o], s_sem.at[1, k - 1, o],
            device_id={"exp": x_at(k)}, device_id_type=MESH,
        )

    def send_t(k):
        return pltpu.make_async_remote_copy(
            t_own.at[k], t_in.at[k - 1], t_sem.at[0, k - 1], t_sem.at[1, k - 1],
            device_id={"ctx": z_at(k)}, device_id_type=MESH,
        )

    def send_up():
        return pltpu.make_async_remote_copy(
            up_out, up_in, up_sem.at[0], up_sem.at[1],
            device_id={"ctx": z_off(GROUP)}, device_id_type=MESH,
        )

    def send_far():
        return pltpu.make_async_remote_copy(
            up_out, far_in, up_sem.at[2], up_sem.at[3],
            device_id={"ctx": z_off(2 * GROUP)}, device_id_type=MESH,
        )

    def send_pz(k):
        return pltpu.make_async_remote_copy(
            pz_out.at[k], pz_in.at[k - 1], pz_sem.at[0, k - 1], pz_sem.at[1, k - 1],
            device_id={"ctx": z_at(k)}, device_id_type=MESH,
        )

    def send_px(q, k):
        return pltpu.make_async_remote_copy(
            px_out.at[q - 1, k], before.at[nx - q, low_at(-k)],
            px_sem.at[0, q - 1, k], px_sem.at[1, q - 1, k],
            device_id={"exp": x_at(q)}, device_id_type=MESH,
        )

    def send_sq(k):
        return pltpu.make_async_remote_copy(
            sq_own, sq_in.at[k - 1], sq_sem.at[0, k - 1], sq_sem.at[1, k - 1],
            device_id={"tp": t_at(k)}, device_id_type=MESH,
        )

    def enter():
        @pl.when(jnp.logical_not(has_down))
        def _():
            pl.semaphore_wait(barrier, partners)

        @pl.when(jnp.logical_and(has_down, jnp.logical_not(takes_far)))
        def _():
            pl.semaphore_wait(barrier, partners + 1)

        @pl.when(takes_far)
        def _():
            pl.semaphore_wait(barrier, partners + 2)
            pl.semaphore_signal(
                far_ok, inc=1, device_id={"ctx": z_off(-2 * GROUP)}, device_id_type=MESH
            )

        @pl.when(has_down)
        def _():
            pl.semaphore_signal(
                up_ok, inc=1, device_id={"ctx": z_off(-GROUP)}, device_id_type=MESH
            )

    position = lax.broadcasted_iota(jnp.int32, (BLK, HEAD_DIM), 0).astype(f32)
    entered = False
    rate_copy.wait()
    for slot in order:
        rate = rate_of(slot)
        load(0, slot).wait()
        load(1, slot).wait()
        tail = jnp.exp(-rate * (BLK - position))
        block_decay = fixed_decay(rate, BLK)
        state = None
        for block in range(blocks):
            at = pl.ds(block * BLK, BLK)
            scaled = (k_buf[slot, at, :].astype(f32) * tail).astype(bf16)
            term = lax.dot_general(
                scaled, v_buf[slot, at, :], (((0,), (0,)), ((), ())), preferred_element_type=f32
            )
            if block < blocks - 1:
                first_term[slot, block] = term
            state = term if state is None else block_decay * state + term
        s_own[slot] = state.reshape(GROUP, slab, HEAD_DIM)
        if not entered:
            enter()
            entered = True
        if slot != 0:
            for o in (3, 2, 1, 0):
                send_s(slot, o).start()

    line = lax.broadcasted_iota(jnp.int32, (BLK, BLK), 0)
    column = lax.broadcasted_iota(jnp.int32, (BLK, BLK), 1)
    causal = line >= column
    spread = jnp.maximum(line - column, 0).astype(f32)
    for slot in range(nx):
        load(2, slot).wait()
        weight = jnp.where(causal, jnp.exp(-rate_of(slot) * spread), 0.0)
        for block in range(blocks):
            at = pl.ds(block * BLK, BLK)
            scores = lax.dot_general(
                q_buf[slot, at, :], k_buf[slot, at, :], (((1,), (1,)), ((), ())),
                preferred_element_type=f32,
            )
            mixing = (scores * weight).astype(bf16)
            att[slot, at, :] = jnp.dot(mixing, v_buf[slot, at, :], preferred_element_type=f32)

    rate = rate_of(0)
    x_weight = [decay(rate, span * (nx - 1 - x_at(-k))) for k in range(nx)]
    z_span = span * nx
    z_weight = [decay(rate, z_span * (GROUP - 1 - low_at(-k))) for k in range(GROUP)]
    for o in (3, 2, 1, 0):
        plane = x_weight[0] * s_own[0, low_at(o)]
        for k in range(1, nx):
            send_s(k, o).wait_recv()
            plane = plane + x_weight[k] * s_in[k - 1, low_at(o)]
        t_own[o] = plane
        if o:
            send_t(o).start()
    whole = z_weight[0] * t_own[0]
    for k in range(1, GROUP):
        send_t(k).wait_recv()
        whole = whole + z_weight[k] * t_in[k - 1]

    slabs = [t_own[0]] + [t_in[k - 1] for k in range(1, GROUP)]
    z_entry = []
    for k in range(GROUP):
        goal = low_at(k)
        z_entry.append(decay(rate, z_span * goal))
        value = None
        for j in range(GROUP):
            if (j + k) % GROUP:
                source = low_at(-j)
                term = decay(rate, z_span * (goal - 1 - source), source < goal) * slabs[j]
                value = term if value is None else value + term
        pz_out[k] = value
    x_entry = []
    for q in range(nx):
        goal = x_at(q)
        x_entry.append(decay(rate, span * goal))
        inner = [decay(rate, span * (goal - 1 - x_at(-j)), x_at(-j) < goal) for j in range(nx)]
        for k in range(GROUP):
            index = low_at(-k)
            value = inner[0] * s_own[0, index]
            for j in range(1, nx):
                value = value + inner[j] * s_in[j - 1, index]
            if q:
                px_out[q - 1, k] = value
            else:
                before[0, index] = value
    group_decay = fixed_decay(rate, z_span * GROUP)

    @pl.when(has_up)
    def _():
        pl.semaphore_wait(up_ok, 1)

    @pl.when(sends_far)
    def _():
        pl.semaphore_wait(far_ok, 1)

    @pl.when(sends_total)
    def _():
        up_out[...] = whole
        send_up().start()

    @pl.when(jnp.logical_not(has_down))
    def _():
        up_in[...] = jnp.zeros_like(up_in)

    @pl.when(has_down)
    def _():
        send_up().wait_recv()

    @pl.when(takes_far)
    def _():
        send_far().wait_recv()
        up_in[...] = up_in[...] + group_decay * far_in[...]

    @pl.when(jnp.logical_and(has_up, jnp.logical_not(sends_total)))
    def _():
        up_out[...] = whole + group_decay * up_in[...]

        @pl.when(sends_far)
        def _():
            send_far().start()

        send_up().start()

    incoming = up_in[...]

    for k in (3, 2, 1, 0):
        pz_out[k] = pz_out[k] + z_entry[k] * incoming
        if k:
            send_pz(k).start()

    for k in range(GROUP):
        if k:
            send_pz(k).wait_recv()
            base = pz_in[k - 1]
        else:
            base = pz_out[0]
        index = low_at(-k)
        for q in (2, 1, 3, 0):
            if q:
                px_out[q - 1, k] = px_out[q - 1, k] + x_entry[q] * base
                send_px(q, k).start()
            else:
                before[0, index] = before[0, index] + x_entry[0] * base

    squares = [jnp.zeros((BLK, HEAD_DIM), f32) for block in range(blocks)]
    for q in (0, 1, 3, 2):
        slot = (nx - q) % nx
        if q:
            for k in range(GROUP):
                pltpu.make_async_remote_copy(
                    px_out.at[q - 1, k], before.at[slot, low_at(-k)],
                    px_sem.at[0, q - 1, k], px_sem.at[1, q - 1, k],
                    device_id={"exp": x_at(q)}, device_id_type=MESH,
                ).wait_recv()
        rate = rate_of(slot)
        inner_decay = jnp.exp(-rate * position)
        block_decay = fixed_decay(rate, BLK)
        state = before[slot].reshape(HEAD_DIM, HEAD_DIM)
        for block in range(blocks):
            at = pl.ds(block * BLK, BLK)
            carried = jnp.dot(
                q_buf[slot, at, :], state.astype(bf16), preferred_element_type=f32
            )
            attended = att[slot, at, :] + carried * inner_decay
            att[slot, at, :] = attended
            squares[block] = squares[block] + attended * attended
            if block < blocks - 1:
                state = block_decay * state + first_term[slot, block]

    pieces = rows // HEAD_DIM
    per_block = BLK // HEAD_DIM
    for c in range(pieces):
        part = squares[c // per_block][(c % per_block) * HEAD_DIM : (c % per_block + 1) * HEAD_DIM]
        sq_own[pl.ds(c, 1), :] = jnp.sum(part.T, axis=0, keepdims=True)
    for k in range(1, nt):
        send_sq(k).start()
    sum_squares = sq_own[...]
    for k in range(1, nt):
        send_sq(k).wait_recv()
        sum_squares = sum_squares + sq_in[k - 1]
    gain_copy.wait()
    scale = lax.rsqrt(sum_squares / (nt * nx * HEAD_DIM) + 1e-06)
    for c in range(pieces):
        at = pl.ds(c * HEAD_DIM, HEAD_DIM)
        row_scale = jnp.broadcast_to(scale[c : c + 1], (HEAD_DIM, HEAD_DIM)).T
        for slot in range(nx):
            head = x_at(slot)
            lanes = pl.ds(pl.multiple_of(head * HEAD_DIM, HEAD_DIM), HEAD_DIM)
            gain = gain_ref[pl.ds(head, 1), :]
            out_ref[at, lanes] = (att[slot, at, :] * row_scale * gain).astype(bf16)

    for k in range(1, nx):
        for c in range(GROUP):
            send_s(k, c).wait_send()
            send_px(k, c).wait_send()
    for k in range(1, GROUP):
        send_t(k).wait_send()
        send_pz(k).wait_send()

    @pl.when(has_up)
    def _():
        send_up().wait_send()

    @pl.when(sends_far)
    def _():
        send_far().wait_send()

    for k in range(1, nt):
        send_sq(k).wait_send()


def solution(mesh):
    nz, nx, nt = mesh.shape["ctx"], mesh.shape["exp"], mesh.shape["tp"]
    slab = HEAD_DIM // GROUP

    def local(queries, key_vectors, value_vectors, decay_rate, norm_gain):
        rows, width = queries.shape
        heads = width // HEAD_DIM
        blocks = rows // BLK
        f32 = jnp.float32
        square = (HEAD_DIM, HEAD_DIM)
        piece = (slab, HEAD_DIM)
        dma = pltpu.SemaphoreType.DMA
        scratch = [
            pltpu.SMEM((heads,), f32),
            pltpu.VMEM((heads, HEAD_DIM), f32),
            pltpu.VMEM((heads, rows, HEAD_DIM), jnp.bfloat16),
            pltpu.VMEM((heads, rows, HEAD_DIM), jnp.bfloat16),
            pltpu.VMEM((heads, rows, HEAD_DIM), jnp.bfloat16),
            pltpu.VMEM((heads, rows, HEAD_DIM), f32),
            pltpu.VMEM((heads, max(blocks - 1, 1)) + square, f32),
            pltpu.VMEM((heads, GROUP) + piece, f32),
            pltpu.VMEM((nx - 1, GROUP) + piece, f32),
            pltpu.VMEM((GROUP,) + piece, f32),
            pltpu.VMEM((GROUP - 1,) + piece, f32),
            pltpu.VMEM(piece, f32),
            pltpu.VMEM(piece, f32),
            pltpu.VMEM(piece, f32),
            pltpu.VMEM((GROUP,) + piece, f32),
            pltpu.VMEM((GROUP - 1,) + piece, f32),
            pltpu.VMEM((nx - 1, GROUP) + piece, f32),
            pltpu.VMEM((heads, GROUP) + piece, f32),
            pltpu.VMEM((rows // HEAD_DIM, HEAD_DIM), f32),
            pltpu.VMEM((nt - 1, rows // HEAD_DIM, HEAD_DIM), f32),
            dma((3, heads)),
            dma,
            dma,
            pltpu.SemaphoreType.REGULAR,
            pltpu.SemaphoreType.REGULAR,
            dma((2, nx - 1, GROUP)),
            dma((2, GROUP - 1)),
            dma((4,)),
            dma((2, GROUP - 1)),
            dma((2, nx - 1, GROUP)),
            dma((2, nt - 1)),
        ]
        return pl.pallas_call(
            functools.partial(kernel, (nz, nx, nt)),
            out_shape=pltpu.VMEM((rows, width), jnp.bfloat16),
            in_specs=[
                pl.BlockSpec(memory_space=pl.ANY),
                pl.BlockSpec(memory_space=pl.ANY),
                pl.BlockSpec(memory_space=pl.ANY),
                pl.BlockSpec(memory_space=pl.ANY),
                pl.BlockSpec(memory_space=pl.ANY),
            ],
            out_specs=pl.BlockSpec(memory_space=pltpu.VMEM),
            scratch_shapes=scratch,
            compiler_params=pltpu.CompilerParams(collective_id=0, has_side_effects=True),
            name="lightning",
        )(queries, key_vectors, value_vectors, decay_rate, norm_gain.reshape(heads, HEAD_DIM))

    return jax.shard_map(
        local,
        mesh=mesh,
        in_specs=(
            P(("ctx", "exp"), "tp"),
            P(("ctx", "exp"), "tp"),
            P(("ctx", "exp"), "tp"),
            P("tp"),
            P("tp"),
        ),
        out_specs=P(("ctx", "exp"), "tp"),
        check_vma=False,
    )
```

```python
import functools

import jax
import jax.numpy as jnp
from jax import lax
from jax.experimental import pallas as pl
from jax.experimental.pallas import tpu as pltpu
from jax.sharding import PartitionSpec as P

HEADS = 32
HEAD_DIM = 128
BLK = 256
GROUP = 4
MESH = pl.DeviceIdType.MESH


def kernel(
    sizes,
    q_hbm,
    k_hbm,
    v_hbm,
    rate_hbm,
    gain_hbm,
    out_ref,
    rate_ref,
    gain_ref,
    q_buf,
    k_buf,
    v_buf,
    att,
    first_term,
    s_own,
    s_in,
    t_own,
    t_in,
    up_out,
    up_in,
    far_in,
    first_in,
    pz_out,
    pz_in,
    px_out,
    before,
    sq_own,
    sq_in,
    load_sem,
    rate_sem,
    gain_sem,
    up_ok,
    far_ok,
    wrap_ok,
    s_sem,
    t_sem,
    up_sem,
    first_sem,
    pz_sem,
    px_sem,
    sq_sem,
):
    nz, nx, nt = sizes
    groups = nz // GROUP
    rows = q_hbm.shape[0]
    blocks = rows // BLK
    span = rows
    slab = HEAD_DIM // GROUP
    f32, bf16 = jnp.float32, jnp.bfloat16

    z, x, t = lax.axis_index("ctx"), lax.axis_index("exp"), lax.axis_index("tp")
    low = lax.rem(z, GROUP)
    high = lax.div(z, GROUP)

    def x_at(k):
        return lax.rem(x + (k + nx), nx)

    def low_at(k):
        return lax.rem(low + (k + GROUP), GROUP)

    def z_at(k):
        return z - low + low_at(k)

    def t_at(k):
        return lax.rem(t + k, nt)

    half = groups // 2
    odd = lax.rem(high, 2) == 1
    has_down, has_up = high > 0, high < groups - 1
    takes_far = jnp.logical_and(odd, high >= half + 1)
    chained = jnp.logical_and(high > 0, has_up)
    relays = jnp.logical_and(high > 0, high < half)
    beyond = list(range(groups - 1, half, -1))
    sends_far = jnp.logical_and(odd, jnp.logical_and(high >= half - 1, high < groups - 2))
    sends_total = jnp.logical_and(jnp.logical_not(odd), high >= half)

    def z_off(k):
        return lax.rem(z + (k + nz), nz)

    barrier = pltpu.get_barrier_semaphore()
    partners = (GROUP - 1) + (nx - 1) + (nt - 1)

    @pl.when(sends_far)
    def _():
        pl.semaphore_signal(
            barrier, inc=1, device_id={"ctx": z_off(2 * GROUP)}, device_id_type=MESH
        )

    @pl.when(has_up)
    def _():
        pl.semaphore_signal(barrier, inc=1, device_id={"ctx": z_off(GROUP)}, device_id_type=MESH)

    @pl.when(high == 0)
    def _():
        for g in beyond:
            pl.semaphore_signal(
                barrier, inc=1, device_id={"ctx": z_off(GROUP * g)}, device_id_type=MESH
            )

    for k in range(1, GROUP):
        pl.semaphore_signal(barrier, inc=1, device_id={"ctx": z_at(k)}, device_id_type=MESH)
    for k in range(1, nx):
        pl.semaphore_signal(barrier, inc=1, device_id={"exp": x_at(k)}, device_id_type=MESH)
    for k in range(1, nt):
        pl.semaphore_signal(barrier, inc=1, device_id={"tp": t_at(k)}, device_id_type=MESH)

    def load(which, slot):
        source, target = ((k_hbm, k_buf), (v_hbm, v_buf), (q_hbm, q_buf))[which]
        lanes = pl.ds(pl.multiple_of(x_at(slot) * HEAD_DIM, HEAD_DIM), HEAD_DIM)
        return pltpu.make_async_copy(
            source.at[:, lanes], target.at[slot], load_sem.at[which, slot]
        )

    rate_copy = pltpu.make_async_copy(rate_hbm, rate_ref, rate_sem)
    gain_copy = pltpu.make_async_copy(gain_hbm, gain_ref, gain_sem)
    rate_copy.start()
    order = [2, 1, 3, 0] if nx == 4 else list(range(1, nx)) + [0]
    for slot in order:
        load(0, slot).start()
        load(1, slot).start()
    for slot in range(nx):
        load(2, slot).start()
    gain_copy.start()

    def rate_of(slot):
        return rate_ref[x_at(slot)]

    def decay(rate, distance, valid=None):
        distance = jnp.maximum(distance, 0)
        weight = jnp.exp(jnp.full((1, HEAD_DIM), -rate * distance.astype(f32), f32))
        if valid is not None:
            weight = weight * jnp.where(valid, 1.0, 0.0).astype(f32)
        return weight

    def fixed_decay(rate, distance):
        return jnp.exp(jnp.full((1, HEAD_DIM), -rate * float(distance), f32))

    def send_s(k, o):
        return pltpu.make_async_remote_copy(
            s_own.at[k, low_at(o)], s_in.at[k - 1, low_at(o)],
            s_sem.at[0, k - 1, o], s_sem.at[1, k - 1, o],
            device_id={"exp": x_at(k)}, device_id_type=MESH,
        )

    def send_t(k):
        return pltpu.make_async_remote_copy(
            t_own.at[k], t_in.at[k - 1], t_sem.at[0, k - 1], t_sem.at[1, k - 1],
            device_id={"ctx": z_at(k)}, device_id_type=MESH,
        )

    def send_up():
        return pltpu.make_async_remote_copy(
            up_out, up_in, up_sem.at[0], up_sem.at[1],
            device_id={"ctx": z_off(GROUP)}, device_id_type=MESH,
        )

    def send_far():
        return pltpu.make_async_remote_copy(
            up_out, far_in, up_sem.at[2], up_sem.at[3],
            device_id={"ctx": z_off(2 * GROUP)}, device_id_type=MESH,
        )

    def send_first(source, g, n):
        return pltpu.make_async_remote_copy(
            source, first_in, first_sem.at[1 + n], first_sem.at[0],
            device_id={"ctx": z_off(GROUP * g)}, device_id_type=MESH,
        )

    def send_pz(k):
        return pltpu.make_async_remote_copy(
            pz_out.at[k], pz_in.at[k - 1], pz_sem.at[0, k - 1], pz_sem.at[1, k - 1],
            device_id={"ctx": z_at(k)}, device_id_type=MESH,
        )

    def send_px(q, k):
        return pltpu.make_async_remote_copy(
            px_out.at[q - 1, k], before.at[nx - q, low_at(-k)],
            px_sem.at[0, q - 1, k], px_sem.at[1, q - 1, k],
            device_id={"exp": x_at(q)}, device_id_type=MESH,
        )

    def send_sq(k):
        return pltpu.make_async_remote_copy(
            sq_own, sq_in.at[k - 1], sq_sem.at[0, k - 1], sq_sem.at[1, k - 1],
            device_id={"tp": t_at(k)}, device_id_type=MESH,
        )

    def enter():
        @pl.when(jnp.logical_not(has_down))
        def _():
            pl.semaphore_wait(barrier, partners)

        @pl.when(jnp.logical_and(has_down, high <= half))
        def _():
            pl.semaphore_wait(barrier, partners + 1)

        @pl.when(jnp.logical_and(high > half, jnp.logical_not(odd)))
        def _():
            pl.semaphore_wait(barrier, partners + 2)

        @pl.when(takes_far)
        def _():
            pl.semaphore_wait(barrier, partners + 3)
            pl.semaphore_signal(
                far_ok, inc=1, device_id={"ctx": z_off(-2 * GROUP)}, device_id_type=MESH
            )

        for n, g in enumerate(beyond):

            @pl.when(high == g)
            def _():
                pl.semaphore_signal(
                    wrap_ok.at[n], inc=1, device_id={"ctx": low}, device_id_type=MESH
                )

        @pl.when(has_down)
        def _():
            pl.semaphore_signal(
                up_ok, inc=1, device_id={"ctx": z_off(-GROUP)}, device_id_type=MESH
            )

    position = lax.broadcasted_iota(jnp.int32, (BLK, HEAD_DIM), 0).astype(f32)
    entered = False
    rate_copy.wait()
    for slot in order:
        rate = rate_of(slot)
        load(0, slot).wait()
        load(1, slot).wait()
        tail = jnp.exp(-rate * (BLK - position))
        block_decay = fixed_decay(rate, BLK)
        state = None
        for block in range(blocks):
            at = pl.ds(block * BLK, BLK)
            scaled = (k_buf[slot, at, :].astype(f32) * tail).astype(bf16)
            term = lax.dot_general(
                scaled, v_buf[slot, at, :], (((0,), (0,)), ((), ())), preferred_element_type=f32
            )
            if block < blocks - 1:
                first_term[slot, block] = term
            state = term if state is None else block_decay * state + term
        s_own[slot] = state.reshape(GROUP, slab, HEAD_DIM)
        if not entered:
            enter()
            entered = True
        if slot != 0:
            for o in (3, 2, 1, 0):
                send_s(slot, o).start()

    line = lax.broadcasted_iota(jnp.int32, (BLK, BLK), 0)
    column = lax.broadcasted_iota(jnp.int32, (BLK, BLK), 1)
    causal = line >= column
    spread = jnp.maximum(line - column, 0).astype(f32)
    for slot in range(nx):
        load(2, slot).wait()
        weight = jnp.where(causal, jnp.exp(-rate_of(slot) * spread), 0.0)
        for block in range(blocks):
            at = pl.ds(block * BLK, BLK)
            scores = lax.dot_general(
                q_buf[slot, at, :], k_buf[slot, at, :], (((1,), (1,)), ((), ())),
                preferred_element_type=f32,
            )
            mixing = (scores * weight).astype(bf16)
            att[slot, at, :] = jnp.dot(mixing, v_buf[slot, at, :], preferred_element_type=f32)

    rate = rate_of(0)
    x_weight = [decay(rate, span * (nx - 1 - x_at(-k))) for k in range(nx)]
    z_span = span * nx
    z_weight = [decay(rate, z_span * (GROUP - 1 - low_at(-k))) for k in range(GROUP)]
    for o in (3, 2, 1, 0):
        plane = x_weight[0] * s_own[0, low_at(o)]
        for k in range(1, nx):
            send_s(k, o).wait_recv()
            plane = plane + x_weight[k] * s_in[k - 1, low_at(o)]
        t_own[o] = plane
        if o:
            send_t(o).start()
    whole = z_weight[0] * t_own[0]
    for k in range(1, GROUP):
        send_t(k).wait_recv()
        whole = whole + z_weight[k] * t_in[k - 1]

    slabs = [t_own[0]] + [t_in[k - 1] for k in range(1, GROUP)]
    z_entry = []
    for k in range(GROUP):
        goal = low_at(k)
        z_entry.append(decay(rate, z_span * goal))
        value = None
        for j in range(GROUP):
            if (j + k) % GROUP:
                source = low_at(-j)
                term = decay(rate, z_span * (goal - 1 - source), source < goal) * slabs[j]
                value = term if value is None else value + term
        pz_out[k] = value
    x_entry = []
    for q in range(nx):
        goal = x_at(q)
        x_entry.append(decay(rate, span * goal))
        inner = [decay(rate, span * (goal - 1 - x_at(-j)), x_at(-j) < goal) for j in range(nx)]
        for k in range(GROUP):
            index = low_at(-k)
            value = inner[0] * s_own[0, index]
            for j in range(1, nx):
                value = value + inner[j] * s_in[j - 1, index]
            if q:
                px_out[q - 1, k] = value
            else:
                before[0, index] = value
    group_decay = fixed_decay(rate, z_span * GROUP)
    first_decay = decay(rate, z_span * GROUP * (high - 1))

    @pl.when(has_up)
    def _():
        pl.semaphore_wait(up_ok, 1)

    @pl.when(sends_far)
    def _():
        pl.semaphore_wait(far_ok, 1)

    @pl.when(sends_total)
    def _():
        up_out[...] = whole
        send_up().start()

    @pl.when(jnp.logical_not(has_down))
    def _():
        up_out[...] = whole
        send_first(up_out, 1, 0).start()
        first_in[...] = jnp.zeros_like(first_in)

    @pl.when(high <= 1)
    def _():
        up_in[...] = jnp.zeros_like(up_in)

    @pl.when(high > 1)
    def _():
        send_up().wait_recv()

    @pl.when(takes_far)
    def _():
        send_far().wait_recv()
        up_in[...] = up_in[...] + group_decay * far_in[...]

    @pl.when(jnp.logical_and(chained, jnp.logical_not(sends_total)))
    def _():
        up_out[...] = whole + group_decay * up_in[...]

        @pl.when(sends_far)
        def _():
            send_far().start()

        send_up().start()

    @pl.when(has_down)
    def _():
        send_first(first_in, 1, 0).wait_recv()

    @pl.when(relays)
    def _():
        send_first(first_in, 1, 0).start()

    incoming = up_in[...] + first_decay * first_in[...]

    for k in (3, 2, 1, 0):
        pz_out[k] = pz_out[k] + z_entry[k] * incoming
        if k:
            send_pz(k).start()

    for k in range(GROUP):
        if k:
            send_pz(k).wait_recv()
            base = pz_in[k - 1]
        else:
            base = pz_out[0]
        index = low_at(-k)
        for q in (2, 1, 3, 0):
            if q:
                px_out[q - 1, k] = px_out[q - 1, k] + x_entry[q] * base
                send_px(q, k).start()
            else:
                before[0, index] = before[0, index] + x_entry[0] * base

    squares = [jnp.zeros((BLK, HEAD_DIM), f32) for block in range(blocks)]
    for q in (0, 1, 3, 2):
        slot = (nx - q) % nx
        if q:
            for k in range(GROUP):
                pltpu.make_async_remote_copy(
                    px_out.at[q - 1, k], before.at[slot, low_at(-k)],
                    px_sem.at[0, q - 1, k], px_sem.at[1, q - 1, k],
                    device_id={"exp": x_at(q)}, device_id_type=MESH,
                ).wait_recv()
        rate = rate_of(slot)
        inner_decay = jnp.exp(-rate * position)
        block_decay = fixed_decay(rate, BLK)
        state = before[slot].reshape(HEAD_DIM, HEAD_DIM)
        for block in range(blocks):
            at = pl.ds(block * BLK, BLK)
            carried = jnp.dot(
                q_buf[slot, at, :], state.astype(bf16), preferred_element_type=f32
            )
            attended = att[slot, at, :] + carried * inner_decay
            att[slot, at, :] = attended
            squares[block] = squares[block] + attended * attended
            if block < blocks - 1:
                state = block_decay * state + first_term[slot, block]

    pieces = rows // HEAD_DIM
    per_block = BLK // HEAD_DIM
    for c in range(pieces):
        part = squares[c // per_block][(c % per_block) * HEAD_DIM : (c % per_block + 1) * HEAD_DIM]
        sq_own[pl.ds(c, 1), :] = jnp.sum(part.T, axis=0, keepdims=True)
    for k in range(1, nt):
        send_sq(k).start()
    sum_squares = sq_own[...]
    for k in range(1, nt):
        send_sq(k).wait_recv()
        sum_squares = sum_squares + sq_in[k - 1]
    gain_copy.wait()
    scale = lax.rsqrt(sum_squares / (nt * nx * HEAD_DIM) + 1e-06)
    for c in range(pieces):
        at = pl.ds(c * HEAD_DIM, HEAD_DIM)
        row_scale = jnp.broadcast_to(scale[c : c + 1], (HEAD_DIM, HEAD_DIM)).T
        for slot in range(nx):
            head = x_at(slot)
            lanes = pl.ds(pl.multiple_of(head * HEAD_DIM, HEAD_DIM), HEAD_DIM)
            gain = gain_ref[pl.ds(head, 1), :]
            out_ref[at, lanes] = (att[slot, at, :] * row_scale * gain).astype(bf16)

    for k in range(1, nx):
        for c in range(GROUP):
            send_s(k, c).wait_send()
            send_px(k, c).wait_send()
    for k in range(1, GROUP):
        send_t(k).wait_send()
        send_pz(k).wait_send()

    @pl.when(jnp.logical_not(has_down))
    def _():
        for n, g in enumerate(beyond):
            pl.semaphore_wait(wrap_ok.at[n], 1)
            send_first(up_out, g, 1 + n).start()
        send_first(up_out, 1, 0).wait_send()
        for n, g in enumerate(beyond):
            send_first(up_out, g, 1 + n).wait_send()

    @pl.when(relays)
    def _():
        send_first(first_in, 1, 0).wait_send()

    @pl.when(chained)
    def _():
        send_up().wait_send()

    @pl.when(sends_far)
    def _():
        send_far().wait_send()

    for k in range(1, nt):
        send_sq(k).wait_send()


def solution(mesh):
    nz, nx, nt = mesh.shape["ctx"], mesh.shape["exp"], mesh.shape["tp"]
    slab = HEAD_DIM // GROUP
    groups = nz // GROUP
    beyond = groups - 1 - groups // 2

    def local(queries, key_vectors, value_vectors, decay_rate, norm_gain):
        rows, width = queries.shape
        heads = width // HEAD_DIM
        blocks = rows // BLK
        f32 = jnp.float32
        square = (HEAD_DIM, HEAD_DIM)
        piece = (slab, HEAD_DIM)
        dma = pltpu.SemaphoreType.DMA
        scratch = [
            pltpu.SMEM((heads,), f32),
            pltpu.VMEM((heads, HEAD_DIM), f32),
            pltpu.VMEM((heads, rows, HEAD_DIM), jnp.bfloat16),
            pltpu.VMEM((heads, rows, HEAD_DIM), jnp.bfloat16),
            pltpu.VMEM((heads, rows, HEAD_DIM), jnp.bfloat16),
            pltpu.VMEM((heads, rows, HEAD_DIM), f32),
            pltpu.VMEM((heads, max(blocks - 1, 1)) + square, f32),
            pltpu.VMEM((heads, GROUP) + piece, f32),
            pltpu.VMEM((nx - 1, GROUP) + piece, f32),
            pltpu.VMEM((GROUP,) + piece, f32),
            pltpu.VMEM((GROUP - 1,) + piece, f32),
            pltpu.VMEM(piece, f32),
            pltpu.VMEM(piece, f32),
            pltpu.VMEM(piece, f32),
            pltpu.VMEM(piece, f32),
            pltpu.VMEM((GROUP,) + piece, f32),
            pltpu.VMEM((GROUP - 1,) + piece, f32),
            pltpu.VMEM((nx - 1, GROUP) + piece, f32),
            pltpu.VMEM((heads, GROUP) + piece, f32),
            pltpu.VMEM((rows // HEAD_DIM, HEAD_DIM), f32),
            pltpu.VMEM((nt - 1, rows // HEAD_DIM, HEAD_DIM), f32),
            dma((3, heads)),
            dma,
            dma,
            pltpu.SemaphoreType.REGULAR,
            pltpu.SemaphoreType.REGULAR,
            pltpu.SemaphoreType.REGULAR((beyond,)),
            dma((2, nx - 1, GROUP)),
            dma((2, GROUP - 1)),
            dma((4,)),
            dma((2 + beyond,)),
            dma((2, GROUP - 1)),
            dma((2, nx - 1, GROUP)),
            dma((2, nt - 1)),
        ]
        return pl.pallas_call(
            functools.partial(kernel, (nz, nx, nt)),
            out_shape=pltpu.VMEM((rows, width), jnp.bfloat16),
            in_specs=[
                pl.BlockSpec(memory_space=pl.ANY),
                pl.BlockSpec(memory_space=pl.ANY),
                pl.BlockSpec(memory_space=pl.ANY),
                pl.BlockSpec(memory_space=pl.ANY),
                pl.BlockSpec(memory_space=pl.ANY),
            ],
            out_specs=pl.BlockSpec(memory_space=pltpu.VMEM),
            scratch_shapes=scratch,
            compiler_params=pltpu.CompilerParams(collective_id=0, has_side_effects=True),
            name="lightning",
        )(queries, key_vectors, value_vectors, decay_rate, norm_gain.reshape(heads, HEAD_DIM))

    return jax.shard_map(
        local,
        mesh=mesh,
        in_specs=(
            P(("ctx", "exp"), "tp"),
            P(("ctx", "exp"), "tp"),
            P(("ctx", "exp"), "tp"),
            P("tp"),
            P("tp"),
        ),
        out_specs=P(("ctx", "exp"), "tp"),
        check_vma=False,
    )
```

```python
import functools

import jax
import jax.numpy as jnp
from jax import lax
from jax.experimental import pallas as pl
from jax.experimental.pallas import tpu as pltpu
from jax.sharding import PartitionSpec as P

HEADS = 32
HEAD_DIM = 128
BLK = 256
GROUP = 4
MESH = pl.DeviceIdType.MESH


def kernel(
    sizes,
    q_hbm,
    k_hbm,
    v_hbm,
    rate_hbm,
    gain_hbm,
    out_ref,
    rate_ref,
    gain_ref,
    q_buf,
    k_buf,
    v_buf,
    att,
    first_term,
    s_own,
    s_in,
    t_own,
    t_in,
    up_out,
    up_in,
    far_in,
    first_in,
    pz_out,
    pz_in,
    px_out,
    before,
    sq_own,
    sq_in,
    load_sem,
    rate_sem,
    gain_sem,
    up_ok,
    far_ok,
    wrap_ok,
    s_sem,
    t_sem,
    up_sem,
    first_sem,
    pz_sem,
    px_sem,
    sq_sem,
):
    nz, nx, nt = sizes
    groups = nz // GROUP
    rows = q_hbm.shape[0]
    blocks = rows // BLK
    span = rows
    slab = HEAD_DIM // GROUP
    f32, bf16 = jnp.float32, jnp.bfloat16

    z, x, t = lax.axis_index("ctx"), lax.axis_index("exp"), lax.axis_index("tp")
    low = lax.rem(z, GROUP)
    high = lax.div(z, GROUP)

    def x_at(k):
        return lax.rem(x + (k + nx), nx)

    def low_at(k):
        return lax.rem(low + (k + GROUP), GROUP)

    def z_at(k):
        return z - low + low_at(k)

    def t_at(k):
        return lax.rem(t + k, nt)

    half = groups // 2
    odd = lax.rem(high, 2) == 1
    has_down, has_up = high > 0, high < groups - 1
    takes_far = jnp.logical_and(odd, high >= half + 1)
    chained = jnp.logical_and(high > 0, has_up)
    relays = jnp.logical_and(high > 0, high <= half)
    beyond = list(range(groups - 1, half + 1, -1))
    sends_far = jnp.logical_and(odd, jnp.logical_and(high >= half - 1, high < groups - 2))
    sends_total = jnp.logical_and(jnp.logical_not(odd), high >= half)

    def z_off(k):
        return lax.rem(z + (k + nz), nz)

    barrier = pltpu.get_barrier_semaphore()
    partners = (GROUP - 1) + (nx - 1) + (nt - 1)

    @pl.when(sends_far)
    def _():
        pl.semaphore_signal(
            barrier, inc=1, device_id={"ctx": z_off(2 * GROUP)}, device_id_type=MESH
        )

    @pl.when(has_up)
    def _():
        pl.semaphore_signal(barrier, inc=1, device_id={"ctx": z_off(GROUP)}, device_id_type=MESH)

    @pl.when(high == 0)
    def _():
        for g in beyond:
            pl.semaphore_signal(
                barrier, inc=1, device_id={"ctx": z_off(GROUP * g)}, device_id_type=MESH
            )

    for k in range(1, GROUP):
        pl.semaphore_signal(barrier, inc=1, device_id={"ctx": z_at(k)}, device_id_type=MESH)
    for k in range(1, nx):
        pl.semaphore_signal(barrier, inc=1, device_id={"exp": x_at(k)}, device_id_type=MESH)
    for k in range(1, nt):
        pl.semaphore_signal(barrier, inc=1, device_id={"tp": t_at(k)}, device_id_type=MESH)

    def load(which, slot):
        source, target = ((k_hbm, k_buf), (v_hbm, v_buf), (q_hbm, q_buf))[which]
        lanes = pl.ds(pl.multiple_of(x_at(slot) * HEAD_DIM, HEAD_DIM), HEAD_DIM)
        return pltpu.make_async_copy(
            source.at[:, lanes], target.at[slot], load_sem.at[which, slot]
        )

    rate_copy = pltpu.make_async_copy(rate_hbm, rate_ref, rate_sem)
    gain_copy = pltpu.make_async_copy(gain_hbm, gain_ref, gain_sem)
    rate_copy.start()
    order = [2, 1, 3, 0] if nx == 4 else list(range(1, nx)) + [0]
    for slot in order:
        load(0, slot).start()
        load(1, slot).start()
    for slot in range(nx):
        load(2, slot).start()
    gain_copy.start()

    def rate_of(slot):
        return rate_ref[x_at(slot)]

    def decay(rate, distance, valid=None):
        distance = jnp.maximum(distance, 0)
        weight = jnp.exp(jnp.full((1, HEAD_DIM), -rate * distance.astype(f32), f32))
        if valid is not None:
            weight = weight * jnp.where(valid, 1.0, 0.0).astype(f32)
        return weight

    def fixed_decay(rate, distance):
        return jnp.exp(jnp.full((1, HEAD_DIM), -rate * float(distance), f32))

    def send_s(k, o):
        return pltpu.make_async_remote_copy(
            s_own.at[k, low_at(o)], s_in.at[k - 1, low_at(o)],
            s_sem.at[0, k - 1, o], s_sem.at[1, k - 1, o],
            device_id={"exp": x_at(k)}, device_id_type=MESH,
        )

    def send_t(k):
        return pltpu.make_async_remote_copy(
            t_own.at[k], t_in.at[k - 1], t_sem.at[0, k - 1], t_sem.at[1, k - 1],
            device_id={"ctx": z_at(k)}, device_id_type=MESH,
        )

    def send_up():
        return pltpu.make_async_remote_copy(
            up_out, up_in, up_sem.at[0], up_sem.at[1],
            device_id={"ctx": z_off(GROUP)}, device_id_type=MESH,
        )

    def send_far():
        return pltpu.make_async_remote_copy(
            up_out, far_in, up_sem.at[2], up_sem.at[3],
            device_id={"ctx": z_off(2 * GROUP)}, device_id_type=MESH,
        )

    def send_first(source, g, n):
        return pltpu.make_async_remote_copy(
            source, first_in, first_sem.at[1 + n], first_sem.at[0],
            device_id={"ctx": z_off(GROUP * g)}, device_id_type=MESH,
        )

    def send_pz(k):
        return pltpu.make_async_remote_copy(
            pz_out.at[k], pz_in.at[k - 1], pz_sem.at[0, k - 1], pz_sem.at[1, k - 1],
            device_id={"ctx": z_at(k)}, device_id_type=MESH,
        )

    def send_px(q, k):
        return pltpu.make_async_remote_copy(
            px_out.at[q - 1, k], before.at[nx - q, low_at(-k)],
            px_sem.at[0, q - 1, k], px_sem.at[1, q - 1, k],
            device_id={"exp": x_at(q)}, device_id_type=MESH,
        )

    def send_sq(k):
        return pltpu.make_async_remote_copy(
            sq_own, sq_in.at[k - 1], sq_sem.at[0, k - 1], sq_sem.at[1, k - 1],
            device_id={"tp": t_at(k)}, device_id_type=MESH,
        )

    def enter():
        below = has_down.astype(jnp.int32) + takes_far + (high > half + 1)
        for n in range(4):

            @pl.when(below == n)
            def _():
                pl.semaphore_wait(barrier, partners + n)

        @pl.when(takes_far)
        def _():
            pl.semaphore_signal(
                far_ok, inc=1, device_id={"ctx": z_off(-2 * GROUP)}, device_id_type=MESH
            )

        for n, g in enumerate(beyond):

            @pl.when(high == g)
            def _():
                pl.semaphore_signal(
                    wrap_ok.at[n], inc=1, device_id={"ctx": low}, device_id_type=MESH
                )

        @pl.when(has_down)
        def _():
            pl.semaphore_signal(
                up_ok, inc=1, device_id={"ctx": z_off(-GROUP)}, device_id_type=MESH
            )

    position = lax.broadcasted_iota(jnp.int32, (BLK, HEAD_DIM), 0).astype(f32)
    rate_copy.wait()
    for slot in order:
        rate = rate_of(slot)
        load(0, slot).wait()
        load(1, slot).wait()
        tail = jnp.exp(-rate * (BLK - position))
        block_decay = fixed_decay(rate, BLK)
        state = None
        for block in range(blocks):
            at = pl.ds(block * BLK, BLK)
            scaled = (k_buf[slot, at, :].astype(f32) * tail).astype(bf16)
            term = lax.dot_general(
                scaled, v_buf[slot, at, :], (((0,), (0,)), ((), ())), preferred_element_type=f32
            )
            if block < blocks - 1:
                first_term[slot, block] = term
            state = term if state is None else block_decay * state + term
        s_own[slot] = state.reshape(GROUP, slab, HEAD_DIM)

    enter()
    for o in (3, 2, 1, 0):
        for slot in order[:-1]:
            send_s(slot, o).start()

    line = lax.broadcasted_iota(jnp.int32, (BLK, BLK), 0)
    column = lax.broadcasted_iota(jnp.int32, (BLK, BLK), 1)
    causal = line >= column
    spread = jnp.maximum(line - column, 0).astype(f32)
    for slot in range(nx):
        load(2, slot).wait()
        weight = jnp.where(causal, jnp.exp(-rate_of(slot) * spread), 0.0)
        for block in range(blocks):
            at = pl.ds(block * BLK, BLK)
            scores = lax.dot_general(
                q_buf[slot, at, :], k_buf[slot, at, :], (((1,), (1,)), ((), ())),
                preferred_element_type=f32,
            )
            mixing = (scores * weight).astype(bf16)
            att[slot, at, :] = jnp.dot(mixing, v_buf[slot, at, :], preferred_element_type=f32)

    rate = rate_of(0)
    x_weight = [decay(rate, span * (nx - 1 - x_at(-k))) for k in range(nx)]
    z_span = span * nx
    z_weight = [decay(rate, z_span * (GROUP - 1 - low_at(-k))) for k in range(GROUP)]
    for o in (3, 2, 1, 0):
        plane = x_weight[0] * s_own[0, low_at(o)]
        for k in range(1, nx):
            send_s(k, o).wait_recv()
            plane = plane + x_weight[k] * s_in[k - 1, low_at(o)]
        t_own[o] = plane
        if o:
            send_t(o).start()
    x_entry = []
    for q in range(nx):
        goal = x_at(q)
        x_entry.append(decay(rate, span * goal))
        inner = [decay(rate, span * (goal - 1 - x_at(-j)), x_at(-j) < goal) for j in range(nx)]
        for k in range(GROUP):
            index = low_at(-k)
            value = inner[0] * s_own[0, index]
            for j in range(1, nx):
                value = value + inner[j] * s_in[j - 1, index]
            if q:
                px_out[q - 1, k] = value
            else:
                before[0, index] = value
    group_decay = fixed_decay(rate, z_span * GROUP)
    first_decay = decay(rate, z_span * GROUP * (high - 1))
    whole = z_weight[0] * t_own[0]
    for k in range(1, GROUP):
        send_t(k).wait_recv()
        whole = whole + z_weight[k] * t_in[k - 1]

    @pl.when(has_up)
    def _():
        pl.semaphore_wait(up_ok, 1)

    @pl.when(sends_far)
    def _():
        pl.semaphore_wait(far_ok, 1)

    @pl.when(sends_total)
    def _():
        up_out[...] = whole
        send_up().start()

    @pl.when(jnp.logical_not(has_down))
    def _():
        up_out[...] = whole
        send_first(up_out, 1, 0).start()
        first_in[...] = jnp.zeros_like(first_in)

    slabs = [t_own[0]] + [t_in[k - 1] for k in range(1, GROUP)]
    z_entry = []
    for k in range(GROUP):
        goal = low_at(k)
        z_entry.append(decay(rate, z_span * goal))
        value = None
        for j in range(GROUP):
            if (j + k) % GROUP:
                source = low_at(-j)
                term = decay(rate, z_span * (goal - 1 - source), source < goal) * slabs[j]
                value = term if value is None else value + term
        pz_out[k] = value

    @pl.when(high <= 1)
    def _():
        up_in[...] = jnp.zeros_like(up_in)

    @pl.when(high > 1)
    def _():
        send_up().wait_recv()

    @pl.when(takes_far)
    def _():
        send_far().wait_recv()
        up_in[...] = up_in[...] + group_decay * far_in[...]

    @pl.when(jnp.logical_and(chained, jnp.logical_not(sends_total)))
    def _():
        up_out[...] = whole + group_decay * up_in[...]

        @pl.when(sends_far)
        def _():
            send_far().start()

        send_up().start()

    @pl.when(has_down)
    def _():
        send_first(first_in, 1, 0).wait_recv()

    @pl.when(relays)
    def _():
        send_first(first_in, 1, 0).start()

    incoming = up_in[...] + first_decay * first_in[...]

    for k in (3, 2, 1, 0):
        pz_out[k] = pz_out[k] + z_entry[k] * incoming
        if k:
            send_pz(k).start()

    for k in range(GROUP):
        if k:
            send_pz(k).wait_recv()
            base = pz_in[k - 1]
        else:
            base = pz_out[0]
        index = low_at(-k)
        for q in (2, 1, 3, 0):
            if q:
                px_out[q - 1, k] = px_out[q - 1, k] + x_entry[q] * base
                send_px(q, k).start()
            else:
                before[0, index] = before[0, index] + x_entry[0] * base

    squares = [jnp.zeros((BLK, HEAD_DIM), f32) for block in range(blocks)]
    for q in (0, 1, 3, 2):
        slot = (nx - q) % nx
        if q:
            for k in range(GROUP):
                pltpu.make_async_remote_copy(
                    px_out.at[q - 1, k], before.at[slot, low_at(-k)],
                    px_sem.at[0, q - 1, k], px_sem.at[1, q - 1, k],
                    device_id={"exp": x_at(q)}, device_id_type=MESH,
                ).wait_recv()
        rate = rate_of(slot)
        inner_decay = jnp.exp(-rate * position)
        block_decay = fixed_decay(rate, BLK)
        state = before[slot].reshape(HEAD_DIM, HEAD_DIM)
        for block in range(blocks):
            at = pl.ds(block * BLK, BLK)
            carried = jnp.dot(
                q_buf[slot, at, :], state.astype(bf16), preferred_element_type=f32
            )
            attended = att[slot, at, :] + carried * inner_decay
            att[slot, at, :] = attended
            squares[block] = squares[block] + attended * attended
            if block < blocks - 1:
                state = block_decay * state + first_term[slot, block]

    pieces = rows // HEAD_DIM
    per_block = BLK // HEAD_DIM
    for c in range(pieces):
        part = squares[c // per_block][(c % per_block) * HEAD_DIM : (c % per_block + 1) * HEAD_DIM]
        sq_own[pl.ds(c, 1), :] = jnp.sum(part.T, axis=0, keepdims=True)
    for k in range(1, nt):
        send_sq(k).start()
    sum_squares = sq_own[...]
    for k in range(1, nt):
        send_sq(k).wait_recv()
        sum_squares = sum_squares + sq_in[k - 1]
    gain_copy.wait()
    scale = lax.rsqrt(sum_squares / (nt * nx * HEAD_DIM) + 1e-06)
    for c in range(pieces):
        at = pl.ds(c * HEAD_DIM, HEAD_DIM)
        row_scale = jnp.broadcast_to(scale[c : c + 1], (HEAD_DIM, HEAD_DIM)).T
        for slot in range(nx):
            head = x_at(slot)
            lanes = pl.ds(pl.multiple_of(head * HEAD_DIM, HEAD_DIM), HEAD_DIM)
            gain = gain_ref[pl.ds(head, 1), :]
            out_ref[at, lanes] = (att[slot, at, :] * row_scale * gain).astype(bf16)

    for k in range(1, nx):
        for c in range(GROUP):
            send_s(k, c).wait_send()
            send_px(k, c).wait_send()
    for k in range(1, GROUP):
        send_t(k).wait_send()
        send_pz(k).wait_send()

    @pl.when(jnp.logical_not(has_down))
    def _():
        for n, g in enumerate(beyond):
            pl.semaphore_wait(wrap_ok.at[n], 1)
            send_first(up_out, g, 1 + n).start()
        send_first(up_out, 1, 0).wait_send()
        for n, g in enumerate(beyond):
            send_first(up_out, g, 1 + n).wait_send()

    @pl.when(relays)
    def _():
        send_first(first_in, 1, 0).wait_send()

    @pl.when(chained)
    def _():
        send_up().wait_send()

    @pl.when(sends_far)
    def _():
        send_far().wait_send()

    for k in range(1, nt):
        send_sq(k).wait_send()


def solution(mesh):
    nz, nx, nt = mesh.shape["ctx"], mesh.shape["exp"], mesh.shape["tp"]
    slab = HEAD_DIM // GROUP
    groups = nz // GROUP
    beyond = max(groups - 2 - groups // 2, 1)

    def local(queries, key_vectors, value_vectors, decay_rate, norm_gain):
        rows, width = queries.shape
        heads = width // HEAD_DIM
        blocks = rows // BLK
        f32 = jnp.float32
        square = (HEAD_DIM, HEAD_DIM)
        piece = (slab, HEAD_DIM)
        dma = pltpu.SemaphoreType.DMA
        scratch = [
            pltpu.SMEM((heads,), f32),
            pltpu.VMEM((heads, HEAD_DIM), f32),
            pltpu.VMEM((heads, rows, HEAD_DIM), jnp.bfloat16),
            pltpu.VMEM((heads, rows, HEAD_DIM), jnp.bfloat16),
            pltpu.VMEM((heads, rows, HEAD_DIM), jnp.bfloat16),
            pltpu.VMEM((heads, rows, HEAD_DIM), f32),
            pltpu.VMEM((heads, max(blocks - 1, 1)) + square, f32),
            pltpu.VMEM((heads, GROUP) + piece, f32),
            pltpu.VMEM((nx - 1, GROUP) + piece, f32),
            pltpu.VMEM((GROUP,) + piece, f32),
            pltpu.VMEM((GROUP - 1,) + piece, f32),
            pltpu.VMEM(piece, f32),
            pltpu.VMEM(piece, f32),
            pltpu.VMEM(piece, f32),
            pltpu.VMEM(piece, f32),
            pltpu.VMEM((GROUP,) + piece, f32),
            pltpu.VMEM((GROUP - 1,) + piece, f32),
            pltpu.VMEM((nx - 1, GROUP) + piece, f32),
            pltpu.VMEM((heads, GROUP) + piece, f32),
            pltpu.VMEM((rows // HEAD_DIM, HEAD_DIM), f32),
            pltpu.VMEM((nt - 1, rows // HEAD_DIM, HEAD_DIM), f32),
            dma((3, heads)),
            dma,
            dma,
            pltpu.SemaphoreType.REGULAR,
            pltpu.SemaphoreType.REGULAR,
            pltpu.SemaphoreType.REGULAR((beyond,)),
            dma((2, nx - 1, GROUP)),
            dma((2, GROUP - 1)),
            dma((4,)),
            dma((2 + beyond,)),
            dma((2, GROUP - 1)),
            dma((2, nx - 1, GROUP)),
            dma((2, nt - 1)),
        ]
        return pl.pallas_call(
            functools.partial(kernel, (nz, nx, nt)),
            out_shape=pltpu.VMEM((rows, width), jnp.bfloat16),
            in_specs=[
                pl.BlockSpec(memory_space=pl.ANY),
                pl.BlockSpec(memory_space=pl.ANY),
                pl.BlockSpec(memory_space=pl.ANY),
                pl.BlockSpec(memory_space=pl.ANY),
                pl.BlockSpec(memory_space=pl.ANY),
            ],
            out_specs=pl.BlockSpec(memory_space=pltpu.VMEM),
            scratch_shapes=scratch,
            compiler_params=pltpu.CompilerParams(collective_id=0, has_side_effects=True),
            name="lightning",
        )(queries, key_vectors, value_vectors, decay_rate, norm_gain.reshape(heads, HEAD_DIM))

    return jax.shard_map(
        local,
        mesh=mesh,
        in_specs=(
            P(("ctx", "exp"), "tp"),
            P(("ctx", "exp"), "tp"),
            P(("ctx", "exp"), "tp"),
            P("tp"),
            P("tp"),
        ),
        out_specs=P(("ctx", "exp"), "tp"),
        check_vma=False,
    )
```

```python
import functools

import jax
import jax.numpy as jnp
from jax import lax
from jax.experimental import pallas as pl
from jax.experimental.pallas import tpu as pltpu
from jax.sharding import PartitionSpec as P

HEADS = 32
HEAD_DIM = 128
BLK = 256
GROUP = 4
MESH = pl.DeviceIdType.MESH


def kernel(
    sizes,
    q_hbm,
    k_hbm,
    v_hbm,
    rate_hbm,
    gain_hbm,
    out_ref,
    rate_ref,
    gain_ref,
    q_buf,
    k_buf,
    v_buf,
    att,
    first_term,
    s_own,
    s_in,
    t_own,
    t_in,
    up_out,
    up_in,
    far_in,
    first_in,
    pz_out,
    pz_in,
    px_out,
    before,
    sq_own,
    sq_in,
    load_sem,
    rate_sem,
    gain_sem,
    up_ok,
    far_ok,
    wrap_ok,
    first_ok,
    s_sem,
    t_sem,
    up_sem,
    first_sem,
    pz_sem,
    px_sem,
    sq_sem,
):
    nz, nx, nt = sizes
    groups = nz // GROUP
    rows = q_hbm.shape[0]
    blocks = rows // BLK
    span = rows
    slab = HEAD_DIM // GROUP
    f32, bf16 = jnp.float32, jnp.bfloat16

    z, x, t = lax.axis_index("ctx"), lax.axis_index("exp"), lax.axis_index("tp")
    low = lax.rem(z, GROUP)
    high = lax.div(z, GROUP)

    def x_at(k):
        return lax.rem(x + (k + nx), nx)

    def low_at(k):
        return lax.rem(low + (k + GROUP), GROUP)

    def z_at(k):
        return z - low + low_at(k)

    def t_at(k):
        return lax.rem(t + k, nt)

    half = groups // 2
    odd = lax.rem(high, 2) == 1
    has_down, has_up = high > 0, high < groups - 1
    takes_far = jnp.logical_and(odd, high >= half + 1)
    chained = jnp.logical_and(high > 0, has_up)
    relays = jnp.logical_and(high > 0, high <= half)
    first_tail = jnp.logical_and(high == 0, low == GROUP - 1)
    second_head = jnp.logical_and(high == 1, low == 0)
    beyond = list(range(groups - 1, half + 1, -1))
    sends_far = jnp.logical_and(odd, jnp.logical_and(high >= half - 1, high < groups - 2))
    sends_total = jnp.logical_and(jnp.logical_not(odd), high >= half)

    def z_off(k):
        return lax.rem(z + (k + nz), nz)

    barrier = pltpu.get_barrier_semaphore()
    partners = (GROUP - 1) + (nx - 1) + (nt - 1)

    @pl.when(sends_far)
    def _():
        pl.semaphore_signal(
            barrier, inc=1, device_id={"ctx": z_off(2 * GROUP)}, device_id_type=MESH
        )

    @pl.when(chained)
    def _():
        pl.semaphore_signal(barrier, inc=1, device_id={"ctx": z_off(GROUP)}, device_id_type=MESH)

    @pl.when(second_head)
    def _():
        pl.semaphore_signal(barrier, inc=1, device_id={"ctx": z_off(-1)}, device_id_type=MESH)

    @pl.when(high == 0)
    def _():
        for g in beyond:
            pl.semaphore_signal(
                barrier, inc=1, device_id={"ctx": z_off(GROUP * g)}, device_id_type=MESH
            )

    for k in range(1, GROUP):
        pl.semaphore_signal(barrier, inc=1, device_id={"ctx": z_at(k)}, device_id_type=MESH)
    for k in range(1, nx):
        pl.semaphore_signal(barrier, inc=1, device_id={"exp": x_at(k)}, device_id_type=MESH)
    for k in range(1, nt):
        pl.semaphore_signal(barrier, inc=1, device_id={"tp": t_at(k)}, device_id_type=MESH)

    def load(which, slot):
        source, target = ((k_hbm, k_buf), (v_hbm, v_buf), (q_hbm, q_buf))[which]
        lanes = pl.ds(pl.multiple_of(x_at(slot) * HEAD_DIM, HEAD_DIM), HEAD_DIM)
        return pltpu.make_async_copy(
            source.at[:, lanes], target.at[slot], load_sem.at[which, slot]
        )

    rate_copy = pltpu.make_async_copy(rate_hbm, rate_ref, rate_sem)
    gain_copy = pltpu.make_async_copy(gain_hbm, gain_ref, gain_sem)
    rate_copy.start()
    order = [2, 1, 3, 0] if nx == 4 else list(range(1, nx)) + [0]
    for slot in order:
        load(0, slot).start()
        load(1, slot).start()
    for slot in range(nx):
        load(2, slot).start()
    gain_copy.start()

    def rate_of(slot):
        return rate_ref[x_at(slot)]

    def decay(rate, distance, valid=None):
        distance = jnp.maximum(distance, 0)
        weight = jnp.exp(jnp.full((1, HEAD_DIM), -rate * distance.astype(f32), f32))
        if valid is not None:
            weight = weight * jnp.where(valid, 1.0, 0.0).astype(f32)
        return weight

    def fixed_decay(rate, distance):
        return jnp.exp(jnp.full((1, HEAD_DIM), -rate * float(distance), f32))

    def send_s(k, o):
        return pltpu.make_async_remote_copy(
            s_own.at[k, low_at(o)], s_in.at[k - 1, low_at(o)],
            s_sem.at[0, k - 1, o], s_sem.at[1, k - 1, o],
            device_id={"exp": x_at(k)}, device_id_type=MESH,
        )

    def send_t(k):
        return pltpu.make_async_remote_copy(
            t_own.at[k], t_in.at[k - 1], t_sem.at[0, k - 1], t_sem.at[1, k - 1],
            device_id={"ctx": z_at(k)}, device_id_type=MESH,
        )

    def send_up():
        return pltpu.make_async_remote_copy(
            up_out, up_in, up_sem.at[0], up_sem.at[1],
            device_id={"ctx": z_off(GROUP)}, device_id_type=MESH,
        )

    def send_far():
        return pltpu.make_async_remote_copy(
            up_out, far_in, up_sem.at[2], up_sem.at[3],
            device_id={"ctx": z_off(2 * GROUP)}, device_id_type=MESH,
        )

    def send_first(source, g, n):
        return pltpu.make_async_remote_copy(
            source, first_in, first_sem.at[1 + n], first_sem.at[0],
            device_id={"ctx": z_off(GROUP * g)}, device_id_type=MESH,
        )

    def send_pz(k):
        return pltpu.make_async_remote_copy(
            pz_out.at[k], pz_in.at[k - 1], pz_sem.at[0, k - 1], pz_sem.at[1, k - 1],
            device_id={"ctx": z_at(k)}, device_id_type=MESH,
        )

    def send_px(q, k):
        return pltpu.make_async_remote_copy(
            px_out.at[q - 1, k], before.at[nx - q, low_at(-k)],
            px_sem.at[0, q - 1, k], px_sem.at[1, q - 1, k],
            device_id={"exp": x_at(q)}, device_id_type=MESH,
        )

    def send_sq(k):
        return pltpu.make_async_remote_copy(
            sq_own, sq_in.at[k - 1], sq_sem.at[0, k - 1], sq_sem.at[1, k - 1],
            device_id={"tp": t_at(k)}, device_id_type=MESH,
        )

    def enter():
        below = (high > 1).astype(jnp.int32) + takes_far + (high > half + 1) + first_tail
        for n in range(4):

            @pl.when(below == n)
            def _():
                pl.semaphore_wait(barrier, partners + n)

        @pl.when(takes_far)
        def _():
            pl.semaphore_signal(
                far_ok, inc=1, device_id={"ctx": z_off(-2 * GROUP)}, device_id_type=MESH
            )

        for n, g in enumerate(beyond):

            @pl.when(high == g)
            def _():
                pl.semaphore_signal(
                    wrap_ok.at[n], inc=1, device_id={"ctx": low}, device_id_type=MESH
                )

        @pl.when(high > 1)
        def _():
            pl.semaphore_signal(
                up_ok, inc=1, device_id={"ctx": z_off(-GROUP)}, device_id_type=MESH
            )

        @pl.when(first_tail)
        def _():
            pl.semaphore_signal(
                first_ok, inc=1, device_id={"ctx": z_off(1)}, device_id_type=MESH
            )

    position = lax.broadcasted_iota(jnp.int32, (BLK, HEAD_DIM), 0).astype(f32)
    rate_copy.wait()
    for slot in order:
        rate = rate_of(slot)
        load(0, slot).wait()
        load(1, slot).wait()
        tail = jnp.exp(-rate * (BLK - position))
        block_decay = fixed_decay(rate, BLK)
        state = None
        for block in range(blocks):
            at = pl.ds(block * BLK, BLK)
            scaled = (k_buf[slot, at, :].astype(f32) * tail).astype(bf16)
            term = lax.dot_general(
                scaled, v_buf[slot, at, :], (((0,), (0,)), ((), ())), preferred_element_type=f32
            )
            if block < blocks - 1:
                first_term[slot, block] = term
            state = term if state is None else block_decay * state + term
        s_own[slot] = state.reshape(GROUP, slab, HEAD_DIM)

    enter()
    for o in (3, 2, 1, 0):
        for slot in order[:-1]:
            send_s(slot, o).start()

    line = lax.broadcasted_iota(jnp.int32, (BLK, BLK), 0)
    column = lax.broadcasted_iota(jnp.int32, (BLK, BLK), 1)
    causal = line >= column
    spread = jnp.maximum(line - column, 0).astype(f32)
    for slot in range(nx):
        load(2, slot).wait()
        weight = jnp.where(causal, jnp.exp(-rate_of(slot) * spread), 0.0)
        for block in range(blocks):
            at = pl.ds(block * BLK, BLK)
            scores = lax.dot_general(
                q_buf[slot, at, :], k_buf[slot, at, :], (((1,), (1,)), ((), ())),
                preferred_element_type=f32,
            )
            mixing = (scores * weight).astype(bf16)
            att[slot, at, :] = jnp.dot(mixing, v_buf[slot, at, :], preferred_element_type=f32)

    rate = rate_of(0)
    x_weight = [decay(rate, span * (nx - 1 - x_at(-k))) for k in range(nx)]
    z_span = span * nx
    z_weight = [decay(rate, z_span * (GROUP - 1 - low_at(-k))) for k in range(GROUP)]
    for o in (3, 2, 1, 0):
        plane = x_weight[0] * s_own[0, low_at(o)]
        for k in range(1, nx):
            send_s(k, o).wait_recv()
            plane = plane + x_weight[k] * s_in[k - 1, low_at(o)]
        t_own[o] = plane
        if o:
            send_t(o).start()

    @pl.when(second_head)
    def _():
        pl.semaphore_wait(first_ok, 1)
        for k in range(1, GROUP + 1):
            pl.semaphore_signal(up_ok, inc=1, device_id={"ctx": z_off(-k)}, device_id_type=MESH)

    x_entry = []
    for q in range(nx):
        goal = x_at(q)
        x_entry.append(decay(rate, span * goal))
        inner = [decay(rate, span * (goal - 1 - x_at(-j)), x_at(-j) < goal) for j in range(nx)]
        for k in range(GROUP):
            index = low_at(-k)
            value = inner[0] * s_own[0, index]
            for j in range(1, nx):
                value = value + inner[j] * s_in[j - 1, index]
            if q:
                px_out[q - 1, k] = value
            else:
                before[0, index] = value
    group_decay = fixed_decay(rate, z_span * GROUP)
    first_decay = decay(rate, z_span * GROUP * (high - 1))
    whole = z_weight[0] * t_own[0]
    for k in range(1, GROUP):
        send_t(k).wait_recv()
        whole = whole + z_weight[k] * t_in[k - 1]

    @pl.when(has_up)
    def _():
        pl.semaphore_wait(up_ok, 1)

    @pl.when(sends_far)
    def _():
        pl.semaphore_wait(far_ok, 1)

    @pl.when(sends_total)
    def _():
        up_out[...] = whole
        send_up().start()

    @pl.when(jnp.logical_not(has_down))
    def _():
        up_out[...] = whole
        send_first(up_out, 1, 0).start()
        first_in[...] = jnp.zeros_like(first_in)

    slabs = [t_own[0]] + [t_in[k - 1] for k in range(1, GROUP)]
    z_entry = []
    for k in range(GROUP):
        goal = low_at(k)
        z_entry.append(decay(rate, z_span * goal))
        value = None
        for j in range(GROUP):
            if (j + k) % GROUP:
                source = low_at(-j)
                term = decay(rate, z_span * (goal - 1 - source), source < goal) * slabs[j]
                value = term if value is None else value + term
        pz_out[k] = value

    @pl.when(high <= 1)
    def _():
        up_in[...] = jnp.zeros_like(up_in)

    @pl.when(high > 1)
    def _():
        send_up().wait_recv()

    @pl.when(takes_far)
    def _():
        send_far().wait_recv()
        up_in[...] = up_in[...] + group_decay * far_in[...]

    @pl.when(jnp.logical_and(chained, jnp.logical_not(sends_total)))
    def _():
        up_out[...] = whole + group_decay * up_in[...]

        @pl.when(sends_far)
        def _():
            send_far().start()

        send_up().start()

    @pl.when(has_down)
    def _():
        send_first(first_in, 1, 0).wait_recv()

    @pl.when(relays)
    def _():
        send_first(first_in, 1, 0).start()

    incoming = up_in[...] + first_decay * first_in[...]

    for k in (3, 2, 1, 0):
        pz_out[k] = pz_out[k] + z_entry[k] * incoming
        if k:
            send_pz(k).start()

    for k in range(GROUP):
        if k:
            send_pz(k).wait_recv()
            base = pz_in[k - 1]
        else:
            base = pz_out[0]
        index = low_at(-k)
        for q in (2, 1, 3, 0):
            if q:
                px_out[q - 1, k] = px_out[q - 1, k] + x_entry[q] * base
                send_px(q, k).start()
            else:
                before[0, index] = before[0, index] + x_entry[0] * base

    squares = [jnp.zeros((BLK, HEAD_DIM), f32) for block in range(blocks)]
    for q in (0, 1, 3, 2):
        slot = (nx - q) % nx
        if q:
            for k in range(GROUP):
                pltpu.make_async_remote_copy(
                    px_out.at[q - 1, k], before.at[slot, low_at(-k)],
                    px_sem.at[0, q - 1, k], px_sem.at[1, q - 1, k],
                    device_id={"exp": x_at(q)}, device_id_type=MESH,
                ).wait_recv()
        rate = rate_of(slot)
        inner_decay = jnp.exp(-rate * position)
        block_decay = fixed_decay(rate, BLK)
        state = before[slot].reshape(HEAD_DIM, HEAD_DIM)
        for block in range(blocks):
            at = pl.ds(block * BLK, BLK)
            carried = jnp.dot(
                q_buf[slot, at, :], state.astype(bf16), preferred_element_type=f32
            )
            attended = att[slot, at, :] + carried * inner_decay
            att[slot, at, :] = attended
            squares[block] = squares[block] + attended * attended
            if block < blocks - 1:
                state = block_decay * state + first_term[slot, block]

    pieces = rows // HEAD_DIM
    per_block = BLK // HEAD_DIM
    for c in range(pieces):
        part = squares[c // per_block][(c % per_block) * HEAD_DIM : (c % per_block + 1) * HEAD_DIM]
        sq_own[pl.ds(c, 1), :] = jnp.sum(part.T, axis=0, keepdims=True)
    for k in range(1, nt):
        send_sq(k).start()
    sum_squares = sq_own[...]
    for k in range(1, nt):
        send_sq(k).wait_recv()
        sum_squares = sum_squares + sq_in[k - 1]
    gain_copy.wait()
    scale = lax.rsqrt(sum_squares / (nt * nx * HEAD_DIM) + 1e-06)
    for c in range(pieces):
        at = pl.ds(c * HEAD_DIM, HEAD_DIM)
        row_scale = jnp.broadcast_to(scale[c : c + 1], (HEAD_DIM, HEAD_DIM)).T
        for slot in range(nx):
            head = x_at(slot)
            lanes = pl.ds(pl.multiple_of(head * HEAD_DIM, HEAD_DIM), HEAD_DIM)
            gain = gain_ref[pl.ds(head, 1), :]
            out_ref[at, lanes] = (att[slot, at, :] * row_scale * gain).astype(bf16)

    for k in range(1, nx):
        for c in range(GROUP):
            send_s(k, c).wait_send()
            send_px(k, c).wait_send()
    for k in range(1, GROUP):
        send_t(k).wait_send()
        send_pz(k).wait_send()

    @pl.when(jnp.logical_not(has_down))
    def _():
        for n, g in enumerate(beyond):
            pl.semaphore_wait(wrap_ok.at[n], 1)
            send_first(up_out, g, 1 + n).start()
        send_first(up_out, 1, 0).wait_send()
        for n, g in enumerate(beyond):
            send_first(up_out, g, 1 + n).wait_send()

    @pl.when(relays)
    def _():
        send_first(first_in, 1, 0).wait_send()

    @pl.when(chained)
    def _():
        send_up().wait_send()

    @pl.when(sends_far)
    def _():
        send_far().wait_send()

    for k in range(1, nt):
        send_sq(k).wait_send()


def solution(mesh):
    nz, nx, nt = mesh.shape["ctx"], mesh.shape["exp"], mesh.shape["tp"]
    slab = HEAD_DIM // GROUP
    groups = nz // GROUP
    beyond = max(groups - 2 - groups // 2, 1)

    def local(queries, key_vectors, value_vectors, decay_rate, norm_gain):
        rows, width = queries.shape
        heads = width // HEAD_DIM
        blocks = rows // BLK
        f32 = jnp.float32
        square = (HEAD_DIM, HEAD_DIM)
        piece = (slab, HEAD_DIM)
        dma = pltpu.SemaphoreType.DMA
        scratch = [
            pltpu.SMEM((heads,), f32),
            pltpu.VMEM((heads, HEAD_DIM), f32),
            pltpu.VMEM((heads, rows, HEAD_DIM), jnp.bfloat16),
            pltpu.VMEM((heads, rows, HEAD_DIM), jnp.bfloat16),
            pltpu.VMEM((heads, rows, HEAD_DIM), jnp.bfloat16),
            pltpu.VMEM((heads, rows, HEAD_DIM), f32),
            pltpu.VMEM((heads, max(blocks - 1, 1)) + square, f32),
            pltpu.VMEM((heads, GROUP) + piece, f32),
            pltpu.VMEM((nx - 1, GROUP) + piece, f32),
            pltpu.VMEM((GROUP,) + piece, f32),
            pltpu.VMEM((GROUP - 1,) + piece, f32),
            pltpu.VMEM(piece, f32),
            pltpu.VMEM(piece, f32),
            pltpu.VMEM(piece, f32),
            pltpu.VMEM(piece, f32),
            pltpu.VMEM((GROUP,) + piece, f32),
            pltpu.VMEM((GROUP - 1,) + piece, f32),
            pltpu.VMEM((nx - 1, GROUP) + piece, f32),
            pltpu.VMEM((heads, GROUP) + piece, f32),
            pltpu.VMEM((rows // HEAD_DIM, HEAD_DIM), f32),
            pltpu.VMEM((nt - 1, rows // HEAD_DIM, HEAD_DIM), f32),
            dma((3, heads)),
            dma,
            dma,
            pltpu.SemaphoreType.REGULAR,
            pltpu.SemaphoreType.REGULAR,
            pltpu.SemaphoreType.REGULAR((beyond,)),
            pltpu.SemaphoreType.REGULAR,
            dma((2, nx - 1, GROUP)),
            dma((2, GROUP - 1)),
            dma((4,)),
            dma((2 + beyond,)),
            dma((2, GROUP - 1)),
            dma((2, nx - 1, GROUP)),
            dma((2, nt - 1)),
        ]
        return pl.pallas_call(
            functools.partial(kernel, (nz, nx, nt)),
            out_shape=pltpu.VMEM((rows, width), jnp.bfloat16),
            in_specs=[
                pl.BlockSpec(memory_space=pl.ANY),
                pl.BlockSpec(memory_space=pl.ANY),
                pl.BlockSpec(memory_space=pl.ANY),
                pl.BlockSpec(memory_space=pl.ANY),
                pl.BlockSpec(memory_space=pl.ANY),
            ],
            out_specs=pl.BlockSpec(memory_space=pltpu.VMEM),
            scratch_shapes=scratch,
            compiler_params=pltpu.CompilerParams(collective_id=0, has_side_effects=True),
            name="lightning",
        )(queries, key_vectors, value_vectors, decay_rate, norm_gain.reshape(heads, HEAD_DIM))

    return jax.shard_map(
        local,
        mesh=mesh,
        in_specs=(
            P(("ctx", "exp"), "tp"),
            P(("ctx", "exp"), "tp"),
            P(("ctx", "exp"), "tp"),
            P("tp"),
            P("tp"),
        ),
        out_specs=P(("ctx", "exp"), "tp"),
        check_vma=False,
    )
```

```python
import functools

import jax
import jax.numpy as jnp
from jax import lax
from jax.experimental import pallas as pl
from jax.experimental.pallas import tpu as pltpu
from jax.sharding import PartitionSpec as P

HEADS = 32
HEAD_DIM = 128
BLK = 256
GROUP = 4
MESH = pl.DeviceIdType.MESH


def kernel(
    sizes,
    q_hbm,
    k_hbm,
    v_hbm,
    rate_hbm,
    gain_hbm,
    out_ref,
    rate_ref,
    gain_ref,
    q_buf,
    k_buf,
    v_buf,
    att,
    first_term,
    s_own,
    s_in,
    t_own,
    t_in,
    up_out,
    up_in,
    far_in,
    first_in,
    pz_out,
    pz_in,
    px_out,
    before,
    sq_own,
    sq_in,
    load_sem,
    rate_sem,
    gain_sem,
    up_ok,
    far_ok,
    wrap_ok,
    first_ok,
    s_sem,
    t_sem,
    up_sem,
    first_sem,
    pz_sem,
    px_sem,
    sq_sem,
):
    nz, nx, nt = sizes
    groups = nz // GROUP
    rows = q_hbm.shape[0]
    blocks = rows // BLK
    span = rows
    slab = HEAD_DIM // GROUP
    f32, bf16 = jnp.float32, jnp.bfloat16

    z, x, t = lax.axis_index("ctx"), lax.axis_index("exp"), lax.axis_index("tp")
    low = lax.rem(z, GROUP)
    high = lax.div(z, GROUP)

    def x_at(k):
        return lax.rem(x + (k + nx), nx)

    def low_at(k):
        return lax.rem(low + (k + GROUP), GROUP)

    def z_at(k):
        return z - low + low_at(k)

    def t_at(k):
        return lax.rem(t + k, nt)

    half = groups // 2
    odd = lax.rem(high, 2) == 1
    has_down, has_up = high > 0, high < groups - 1
    takes_far = jnp.logical_and(odd, high >= half + 1)
    chained = jnp.logical_and(high > 0, has_up)
    relays = jnp.logical_and(odd, high <= half)
    relays_far = jnp.logical_and(odd, high <= half - 1)
    hears_far = jnp.logical_and(odd, high >= 3)
    heard_far = jnp.logical_and(odd, high < groups - 2)
    first_tail = jnp.logical_and(high == 0, low == GROUP - 1)
    second_head = jnp.logical_and(high == 1, low == 0)
    beyond = list(range(groups - 1, half + 1, -1))
    sends_far = jnp.logical_and(odd, jnp.logical_and(high >= half - 1, high < groups - 2))
    sends_total = jnp.logical_and(jnp.logical_not(odd), high >= half)

    def z_off(k):
        return lax.rem(z + (k + nz), nz)

    barrier = pltpu.get_barrier_semaphore()
    partners = (GROUP - 1) + (nx - 1) + (nt - 1)

    @pl.when(heard_far)
    def _():
        pl.semaphore_signal(
            barrier, inc=1, device_id={"ctx": z_off(2 * GROUP)}, device_id_type=MESH
        )

    @pl.when(chained)
    def _():
        pl.semaphore_signal(barrier, inc=1, device_id={"ctx": z_off(GROUP)}, device_id_type=MESH)

    @pl.when(second_head)
    def _():
        pl.semaphore_signal(barrier, inc=1, device_id={"ctx": z_off(-1)}, device_id_type=MESH)

    @pl.when(high == 0)
    def _():
        for g in beyond:
            pl.semaphore_signal(
                barrier, inc=1, device_id={"ctx": z_off(GROUP * g)}, device_id_type=MESH
            )

    for k in range(1, GROUP):
        pl.semaphore_signal(barrier, inc=1, device_id={"ctx": z_at(k)}, device_id_type=MESH)
    for k in range(1, nx):
        pl.semaphore_signal(barrier, inc=1, device_id={"exp": x_at(k)}, device_id_type=MESH)
    for k in range(1, nt):
        pl.semaphore_signal(barrier, inc=1, device_id={"tp": t_at(k)}, device_id_type=MESH)

    def load(which, slot):
        source, target = ((k_hbm, k_buf), (v_hbm, v_buf), (q_hbm, q_buf))[which]
        lanes = pl.ds(pl.multiple_of(x_at(slot) * HEAD_DIM, HEAD_DIM), HEAD_DIM)
        return pltpu.make_async_copy(
            source.at[:, lanes], target.at[slot], load_sem.at[which, slot]
        )

    rate_copy = pltpu.make_async_copy(rate_hbm, rate_ref, rate_sem)
    gain_copy = pltpu.make_async_copy(gain_hbm, gain_ref, gain_sem)
    rate_copy.start()
    order = [2, 1, 3, 0] if nx == 4 else list(range(1, nx)) + [0]
    for slot in order:
        load(0, slot).start()
        load(1, slot).start()
    for slot in range(nx):
        load(2, slot).start()
    gain_copy.start()

    def rate_of(slot):
        return rate_ref[x_at(slot)]

    def decay(rate, distance, valid=None):
        distance = jnp.maximum(distance, 0)
        weight = jnp.exp(jnp.full((1, HEAD_DIM), -rate * distance.astype(f32), f32))
        if valid is not None:
            weight = weight * jnp.where(valid, 1.0, 0.0).astype(f32)
        return weight

    def fixed_decay(rate, distance):
        return jnp.exp(jnp.full((1, HEAD_DIM), -rate * float(distance), f32))

    def send_s(k, o):
        return pltpu.make_async_remote_copy(
            s_own.at[k, low_at(o)], s_in.at[k - 1, low_at(o)],
            s_sem.at[0, k - 1, o], s_sem.at[1, k - 1, o],
            device_id={"exp": x_at(k)}, device_id_type=MESH,
        )

    def send_t(k):
        return pltpu.make_async_remote_copy(
            t_own.at[k], t_in.at[k - 1], t_sem.at[0, k - 1], t_sem.at[1, k - 1],
            device_id={"ctx": z_at(k)}, device_id_type=MESH,
        )

    def send_up():
        return pltpu.make_async_remote_copy(
            up_out, up_in, up_sem.at[0], up_sem.at[1],
            device_id={"ctx": z_off(GROUP)}, device_id_type=MESH,
        )

    def send_far():
        return pltpu.make_async_remote_copy(
            up_out, far_in, up_sem.at[2], up_sem.at[3],
            device_id={"ctx": z_off(2 * GROUP)}, device_id_type=MESH,
        )

    def send_first(source, g, n):
        return pltpu.make_async_remote_copy(
            source, first_in, first_sem.at[1 + n], first_sem.at[0],
            device_id={"ctx": z_off(GROUP * g)}, device_id_type=MESH,
        )

    def send_pz(k):
        return pltpu.make_async_remote_copy(
            pz_out.at[k], pz_in.at[k - 1], pz_sem.at[0, k - 1], pz_sem.at[1, k - 1],
            device_id={"ctx": z_at(k)}, device_id_type=MESH,
        )

    def send_px(q, k):
        return pltpu.make_async_remote_copy(
            px_out.at[q - 1, k], before.at[nx - q, low_at(-k)],
            px_sem.at[0, q - 1, k], px_sem.at[1, q - 1, k],
            device_id={"exp": x_at(q)}, device_id_type=MESH,
        )

    def send_sq(k):
        return pltpu.make_async_remote_copy(
            sq_own, sq_in.at[k - 1], sq_sem.at[0, k - 1], sq_sem.at[1, k - 1],
            device_id={"tp": t_at(k)}, device_id_type=MESH,
        )

    def enter():
        below = (high > 1).astype(jnp.int32) + hears_far + (high > half + 1) + first_tail
        for n in range(4):

            @pl.when(below == n)
            def _():
                pl.semaphore_wait(barrier, partners + n)

        @pl.when(hears_far)
        def _():
            pl.semaphore_signal(
                far_ok, inc=1, device_id={"ctx": z_off(-2 * GROUP)}, device_id_type=MESH
            )

        for n, g in enumerate(beyond):

            @pl.when(high == g)
            def _():
                pl.semaphore_signal(
                    wrap_ok.at[n], inc=1, device_id={"ctx": low}, device_id_type=MESH
                )

        @pl.when(high > 1)
        def _():
            pl.semaphore_signal(
                up_ok, inc=1, device_id={"ctx": z_off(-GROUP)}, device_id_type=MESH
            )

        @pl.when(first_tail)
        def _():
            pl.semaphore_signal(
                first_ok, inc=1, device_id={"ctx": z_off(1)}, device_id_type=MESH
            )

    position = lax.broadcasted_iota(jnp.int32, (BLK, HEAD_DIM), 0).astype(f32)
    rate_copy.wait()
    for slot in order:
        rate = rate_of(slot)
        load(0, slot).wait()
        load(1, slot).wait()
        tail = jnp.exp(-rate * (BLK - position))
        block_decay = fixed_decay(rate, BLK)
        state = None
        for block in range(blocks):
            at = pl.ds(block * BLK, BLK)
            scaled = (k_buf[slot, at, :].astype(f32) * tail).astype(bf16)
            term = lax.dot_general(
                scaled, v_buf[slot, at, :], (((0,), (0,)), ((), ())), preferred_element_type=f32
            )
            if block < blocks - 1:
                first_term[slot, block] = term
            state = term if state is None else block_decay * state + term
        s_own[slot] = state.reshape(GROUP, slab, HEAD_DIM)

    enter()
    for o in (3, 2, 1, 0):
        for slot in order[:-1]:
            send_s(slot, o).start()

    line = lax.broadcasted_iota(jnp.int32, (BLK, BLK), 0)
    column = lax.broadcasted_iota(jnp.int32, (BLK, BLK), 1)
    causal = line >= column
    spread = jnp.maximum(line - column, 0).astype(f32)
    for slot in range(nx):
        load(2, slot).wait()
        weight = jnp.where(causal, jnp.exp(-rate_of(slot) * spread), 0.0)
        for block in range(blocks):
            at = pl.ds(block * BLK, BLK)
            scores = lax.dot_general(
                q_buf[slot, at, :], k_buf[slot, at, :], (((1,), (1,)), ((), ())),
                preferred_element_type=f32,
            )
            mixing = (scores * weight).astype(bf16)
            att[slot, at, :] = jnp.dot(mixing, v_buf[slot, at, :], preferred_element_type=f32)

    rate = rate_of(0)
    x_weight = [decay(rate, span * (nx - 1 - x_at(-k))) for k in range(nx)]
    z_span = span * nx
    z_weight = [decay(rate, z_span * (GROUP - 1 - low_at(-k))) for k in range(GROUP)]
    for o in (3, 2, 1, 0):
        plane = x_weight[0] * s_own[0, low_at(o)]
        for k in range(1, nx):
            send_s(k, o).wait_recv()
            plane = plane + x_weight[k] * s_in[k - 1, low_at(o)]
        t_own[o] = plane
        if o:
            send_t(o).start()

    @pl.when(second_head)
    def _():
        pl.semaphore_wait(first_ok, 1)
        for k in range(1, GROUP + 1):
            pl.semaphore_signal(up_ok, inc=1, device_id={"ctx": z_off(-k)}, device_id_type=MESH)

    x_entry = []
    for q in range(nx):
        goal = x_at(q)
        x_entry.append(decay(rate, span * goal))
        inner = [decay(rate, span * (goal - 1 - x_at(-j)), x_at(-j) < goal) for j in range(nx)]
        for k in range(GROUP):
            index = low_at(-k)
            value = inner[0] * s_own[0, index]
            for j in range(1, nx):
                value = value + inner[j] * s_in[j - 1, index]
            if q:
                px_out[q - 1, k] = value
            else:
                before[0, index] = value
    group_decay = fixed_decay(rate, z_span * GROUP)
    first_decay = decay(rate, z_span * GROUP * (high - 1))
    whole = z_weight[0] * t_own[0]
    for k in range(1, GROUP):
        send_t(k).wait_recv()
        whole = whole + z_weight[k] * t_in[k - 1]

    @pl.when(has_up)
    def _():
        pl.semaphore_wait(up_ok, 1)

    @pl.when(sends_far)
    def _():
        pl.semaphore_wait(far_ok, 1)

    @pl.when(sends_total)
    def _():
        up_out[...] = whole
        send_up().start()

    @pl.when(jnp.logical_not(has_down))
    def _():
        up_out[...] = whole
        send_first(up_out, 1, 0).start()
        first_in[...] = jnp.zeros_like(first_in)

    slabs = [t_own[0]] + [t_in[k - 1] for k in range(1, GROUP)]
    z_entry = []
    for k in range(GROUP):
        goal = low_at(k)
        z_entry.append(decay(rate, z_span * goal))
        value = None
        for j in range(GROUP):
            if (j + k) % GROUP:
                source = low_at(-j)
                term = decay(rate, z_span * (goal - 1 - source), source < goal) * slabs[j]
                value = term if value is None else value + term
        pz_out[k] = value

    @pl.when(high <= 1)
    def _():
        up_in[...] = jnp.zeros_like(up_in)

    @pl.when(high > 1)
    def _():
        send_up().wait_recv()

    @pl.when(takes_far)
    def _():
        send_far().wait_recv()
        up_in[...] = up_in[...] + group_decay * far_in[...]

    @pl.when(jnp.logical_and(chained, jnp.logical_not(sends_total)))
    def _():
        up_out[...] = whole + group_decay * up_in[...]

        @pl.when(sends_far)
        def _():
            send_far().start()

        send_up().start()

    @pl.when(has_down)
    def _():
        send_first(first_in, 1, 0).wait_recv()

    @pl.when(jnp.logical_and(relays_far, jnp.logical_not(sends_far)))
    def _():
        pl.semaphore_wait(far_ok, 1)

    @pl.when(relays_far)
    def _():
        send_first(first_in, 2, 1 + len(beyond)).start()

    @pl.when(relays)
    def _():
        send_first(first_in, 1, 0).start()

    incoming = up_in[...] + first_decay * first_in[...]

    for k in (3, 2, 1, 0):
        pz_out[k] = pz_out[k] + z_entry[k] * incoming
        if k:
            send_pz(k).start()

    for k in range(GROUP):
        if k:
            send_pz(k).wait_recv()
            base = pz_in[k - 1]
        else:
            base = pz_out[0]
        index = low_at(-k)
        for q in (2, 1, 3, 0):
            if q:
                px_out[q - 1, k] = px_out[q - 1, k] + x_entry[q] * base
                send_px(q, k).start()
            else:
                before[0, index] = before[0, index] + x_entry[0] * base

    squares = [jnp.zeros((BLK, HEAD_DIM), f32) for block in range(blocks)]
    for q in (0, 1, 3, 2):
        slot = (nx - q) % nx
        if q:
            for k in range(GROUP):
                pltpu.make_async_remote_copy(
                    px_out.at[q - 1, k], before.at[slot, low_at(-k)],
                    px_sem.at[0, q - 1, k], px_sem.at[1, q - 1, k],
                    device_id={"exp": x_at(q)}, device_id_type=MESH,
                ).wait_recv()
        rate = rate_of(slot)
        inner_decay = jnp.exp(-rate * position)
        block_decay = fixed_decay(rate, BLK)
        state = before[slot].reshape(HEAD_DIM, HEAD_DIM)
        for block in range(blocks):
            at = pl.ds(block * BLK, BLK)
            carried = jnp.dot(
                q_buf[slot, at, :], state.astype(bf16), preferred_element_type=f32
            )
            attended = att[slot, at, :] + carried * inner_decay
            att[slot, at, :] = attended
            squares[block] = squares[block] + attended * attended
            if block < blocks - 1:
                state = block_decay * state + first_term[slot, block]

    pieces = rows // HEAD_DIM
    per_block = BLK // HEAD_DIM
    for c in range(pieces):
        part = squares[c // per_block][(c % per_block) * HEAD_DIM : (c % per_block + 1) * HEAD_DIM]
        sq_own[pl.ds(c, 1), :] = jnp.sum(part.T, axis=0, keepdims=True)
    for k in range(1, nt):
        send_sq(k).start()
    sum_squares = sq_own[...]
    for k in range(1, nt):
        send_sq(k).wait_recv()
        sum_squares = sum_squares + sq_in[k - 1]
    gain_copy.wait()
    scale = lax.rsqrt(sum_squares / (nt * nx * HEAD_DIM) + 1e-06)
    for c in range(pieces):
        at = pl.ds(c * HEAD_DIM, HEAD_DIM)
        row_scale = jnp.broadcast_to(scale[c : c + 1], (HEAD_DIM, HEAD_DIM)).T
        for slot in range(nx):
            head = x_at(slot)
            lanes = pl.ds(pl.multiple_of(head * HEAD_DIM, HEAD_DIM), HEAD_DIM)
            gain = gain_ref[pl.ds(head, 1), :]
            out_ref[at, lanes] = (att[slot, at, :] * row_scale * gain).astype(bf16)

    for k in range(1, nx):
        for c in range(GROUP):
            send_s(k, c).wait_send()
            send_px(k, c).wait_send()
    for k in range(1, GROUP):
        send_t(k).wait_send()
        send_pz(k).wait_send()

    @pl.when(jnp.logical_not(has_down))
    def _():
        for n, g in enumerate(beyond):
            pl.semaphore_wait(wrap_ok.at[n], 1)
            send_first(up_out, g, 1 + n).start()
        send_first(up_out, 1, 0).wait_send()
        for n, g in enumerate(beyond):
            send_first(up_out, g, 1 + n).wait_send()

    @pl.when(relays)
    def _():
        send_first(first_in, 1, 0).wait_send()

    @pl.when(relays_far)
    def _():
        send_first(first_in, 2, 1 + len(beyond)).wait_send()

    @pl.when(chained)
    def _():
        send_up().wait_send()

    @pl.when(sends_far)
    def _():
        send_far().wait_send()

    for k in range(1, nt):
        send_sq(k).wait_send()


def solution(mesh):
    nz, nx, nt = mesh.shape["ctx"], mesh.shape["exp"], mesh.shape["tp"]
    slab = HEAD_DIM // GROUP
    groups = nz // GROUP
    beyond = max(groups - 2 - groups // 2, 1)

    def local(queries, key_vectors, value_vectors, decay_rate, norm_gain):
        rows, width = queries.shape
        heads = width // HEAD_DIM
        blocks = rows // BLK
        f32 = jnp.float32
        square = (HEAD_DIM, HEAD_DIM)
        piece = (slab, HEAD_DIM)
        dma = pltpu.SemaphoreType.DMA
        scratch = [
            pltpu.SMEM((heads,), f32),
            pltpu.VMEM((heads, HEAD_DIM), f32),
            pltpu.VMEM((heads, rows, HEAD_DIM), jnp.bfloat16),
            pltpu.VMEM((heads, rows, HEAD_DIM), jnp.bfloat16),
            pltpu.VMEM((heads, rows, HEAD_DIM), jnp.bfloat16),
            pltpu.VMEM((heads, rows, HEAD_DIM), f32),
            pltpu.VMEM((heads, max(blocks - 1, 1)) + square, f32),
            pltpu.VMEM((heads, GROUP) + piece, f32),
            pltpu.VMEM((nx - 1, GROUP) + piece, f32),
            pltpu.VMEM((GROUP,) + piece, f32),
            pltpu.VMEM((GROUP - 1,) + piece, f32),
            pltpu.VMEM(piece, f32),
            pltpu.VMEM(piece, f32),
            pltpu.VMEM(piece, f32),
            pltpu.VMEM(piece, f32),
            pltpu.VMEM((GROUP,) + piece, f32),
            pltpu.VMEM((GROUP - 1,) + piece, f32),
            pltpu.VMEM((nx - 1, GROUP) + piece, f32),
            pltpu.VMEM((heads, GROUP) + piece, f32),
            pltpu.VMEM((rows // HEAD_DIM, HEAD_DIM), f32),
            pltpu.VMEM((nt - 1, rows // HEAD_DIM, HEAD_DIM), f32),
            dma((3, heads)),
            dma,
            dma,
            pltpu.SemaphoreType.REGULAR,
            pltpu.SemaphoreType.REGULAR,
            pltpu.SemaphoreType.REGULAR((beyond,)),
            pltpu.SemaphoreType.REGULAR,
            dma((2, nx - 1, GROUP)),
            dma((2, GROUP - 1)),
            dma((4,)),
            dma((3 + beyond,)),
            dma((2, GROUP - 1)),
            dma((2, nx - 1, GROUP)),
            dma((2, nt - 1)),
        ]
        return pl.pallas_call(
            functools.partial(kernel, (nz, nx, nt)),
            out_shape=pltpu.VMEM((rows, width), jnp.bfloat16),
            in_specs=[
                pl.BlockSpec(memory_space=pl.ANY),
                pl.BlockSpec(memory_space=pl.ANY),
                pl.BlockSpec(memory_space=pl.ANY),
                pl.BlockSpec(memory_space=pl.ANY),
                pl.BlockSpec(memory_space=pl.ANY),
            ],
            out_specs=pl.BlockSpec(memory_space=pltpu.VMEM),
            scratch_shapes=scratch,
            compiler_params=pltpu.CompilerParams(collective_id=0, has_side_effects=True),
            name="lightning",
        )(queries, key_vectors, value_vectors, decay_rate, norm_gain.reshape(heads, HEAD_DIM))

    return jax.shard_map(
        local,
        mesh=mesh,
        in_specs=(
            P(("ctx", "exp"), "tp"),
            P(("ctx", "exp"), "tp"),
            P(("ctx", "exp"), "tp"),
            P("tp"),
            P("tp"),
        ),
        out_specs=P(("ctx", "exp"), "tp"),
        check_vma=False,
    )
```

```python
import functools

import jax
import jax.numpy as jnp
from jax import lax
from jax.experimental import pallas as pl
from jax.experimental.pallas import tpu as pltpu
from jax.sharding import PartitionSpec as P

HEADS = 32
HEAD_DIM = 128
BLK = 256
GROUP = 4
MESH = pl.DeviceIdType.MESH


def kernel(
    sizes,
    q_hbm,
    k_hbm,
    v_hbm,
    rate_hbm,
    gain_hbm,
    out_ref,
    rate_ref,
    gain_ref,
    q_buf,
    k_buf,
    v_buf,
    att,
    first_term,
    s_own,
    s_in,
    t_own,
    t_in,
    up_out,
    up_in,
    far_in,
    first_in,
    pz_out,
    pz_in,
    px_out,
    before,
    sq_own,
    sq_in,
    load_sem,
    rate_sem,
    gain_sem,
    up_ok,
    far_ok,
    wrap_ok,
    first_ok,
    s_sem,
    t_sem,
    up_sem,
    first_sem,
    pz_sem,
    px_sem,
    sq_sem,
):
    nz, nx, nt = sizes
    groups = nz // GROUP
    rows = q_hbm.shape[0]
    blocks = rows // BLK
    span = rows
    slab = HEAD_DIM // GROUP
    f32, bf16 = jnp.float32, jnp.bfloat16

    z, x, t = lax.axis_index("ctx"), lax.axis_index("exp"), lax.axis_index("tp")
    low = lax.rem(z, GROUP)
    high = lax.div(z, GROUP)

    def x_at(k):
        return lax.rem(x + (k + nx), nx)

    def low_at(k):
        return lax.rem(low + (k + GROUP), GROUP)

    def z_at(k):
        return z - low + low_at(k)

    def t_at(k):
        return lax.rem(t + k, nt)

    half = groups // 2
    odd = lax.rem(high, 2) == 1
    has_down, has_up = high > 0, high < groups - 1
    takes_far = jnp.logical_and(odd, high >= half + 1)
    chained = jnp.logical_and(high > 0, has_up)
    relays = jnp.logical_and(odd, high <= half)
    relays_far = jnp.logical_and(odd, high <= half - 1)
    hears_far = jnp.logical_and(odd, high >= 3)
    heard_far = jnp.logical_and(odd, high < groups - 2)
    first_tail = jnp.logical_and(high == 0, low == GROUP - 1)
    second_head = jnp.logical_and(high == 1, low == 0)
    beyond = list(range(groups - 1, half + 1, -1))
    sends_far = jnp.logical_and(odd, jnp.logical_and(high >= half - 1, high < groups - 2))
    sends_total = jnp.logical_and(jnp.logical_not(odd), high >= half)

    def z_off(k):
        return lax.rem(z + (k + nz), nz)

    barrier = pltpu.get_barrier_semaphore()
    partners = (GROUP - 1) + (nx - 1) + (nt - 1)

    @pl.when(heard_far)
    def _():
        pl.semaphore_signal(
            barrier, inc=1, device_id={"ctx": z_off(2 * GROUP)}, device_id_type=MESH
        )

    @pl.when(chained)
    def _():
        pl.semaphore_signal(barrier, inc=1, device_id={"ctx": z_off(GROUP)}, device_id_type=MESH)

    @pl.when(second_head)
    def _():
        pl.semaphore_signal(barrier, inc=1, device_id={"ctx": z_off(-1)}, device_id_type=MESH)

    @pl.when(high == 0)
    def _():
        for g in beyond:
            pl.semaphore_signal(
                barrier, inc=1, device_id={"ctx": z_off(GROUP * g)}, device_id_type=MESH
            )

    for k in range(1, GROUP):
        pl.semaphore_signal(barrier, inc=1, device_id={"ctx": z_at(k)}, device_id_type=MESH)
    for k in range(1, nx):
        pl.semaphore_signal(barrier, inc=1, device_id={"exp": x_at(k)}, device_id_type=MESH)
    for k in range(1, nt):
        pl.semaphore_signal(barrier, inc=1, device_id={"tp": t_at(k)}, device_id_type=MESH)

    def load(which, slot):
        source, target = ((k_hbm, k_buf), (v_hbm, v_buf), (q_hbm, q_buf))[which]
        lanes = pl.ds(pl.multiple_of(x_at(slot) * HEAD_DIM, HEAD_DIM), HEAD_DIM)
        return pltpu.make_async_copy(
            source.at[:, lanes], target.at[slot], load_sem.at[which, slot]
        )

    rate_copy = pltpu.make_async_copy(rate_hbm, rate_ref, rate_sem)
    gain_copy = pltpu.make_async_copy(gain_hbm, gain_ref, gain_sem)
    rate_copy.start()
    order = [2, 1, 3, 0] if nx == 4 else list(range(1, nx)) + [0]
    for slot in order:
        load(0, slot).start()
        load(1, slot).start()
    for slot in range(nx):
        load(2, slot).start()
    gain_copy.start()

    def rate_of(slot):
        return rate_ref[x_at(slot)]

    def decay(rate, distance, valid=None):
        distance = jnp.maximum(distance, 0)
        weight = jnp.exp(jnp.full((1, HEAD_DIM), -rate * distance.astype(f32), f32))
        if valid is not None:
            weight = weight * jnp.where(valid, 1.0, 0.0).astype(f32)
        return weight

    def fixed_decay(rate, distance):
        return jnp.exp(jnp.full((1, HEAD_DIM), -rate * float(distance), f32))

    def send_s(k, o):
        return pltpu.make_async_remote_copy(
            s_own.at[k, low_at(o)], s_in.at[k - 1, low_at(o)],
            s_sem.at[0, k - 1, o], s_sem.at[1, k - 1, o],
            device_id={"exp": x_at(k)}, device_id_type=MESH,
        )

    def send_t(k):
        return pltpu.make_async_remote_copy(
            t_own.at[k], t_in.at[k - 1], t_sem.at[0, k - 1], t_sem.at[1, k - 1],
            device_id={"ctx": z_at(k)}, device_id_type=MESH,
        )

    def send_up():
        return pltpu.make_async_remote_copy(
            up_out, up_in, up_sem.at[0], up_sem.at[1],
            device_id={"ctx": z_off(GROUP)}, device_id_type=MESH,
        )

    def send_far():
        return pltpu.make_async_remote_copy(
            up_out, far_in, up_sem.at[2], up_sem.at[3],
            device_id={"ctx": z_off(2 * GROUP)}, device_id_type=MESH,
        )

    def send_first(source, g, n):
        return pltpu.make_async_remote_copy(
            source, first_in, first_sem.at[1 + n], first_sem.at[0],
            device_id={"ctx": z_off(GROUP * g)}, device_id_type=MESH,
        )

    def send_pz(k):
        return pltpu.make_async_remote_copy(
            pz_out.at[k], pz_in.at[k - 1], pz_sem.at[0, k - 1], pz_sem.at[1, k - 1],
            device_id={"ctx": z_at(k)}, device_id_type=MESH,
        )

    def send_px(q, k):
        return pltpu.make_async_remote_copy(
            px_out.at[q - 1, k], before.at[nx - q, low_at(-k)],
            px_sem.at[0, q - 1, k], px_sem.at[1, q - 1, k],
            device_id={"exp": x_at(q)}, device_id_type=MESH,
        )

    def send_sq(k):
        return pltpu.make_async_remote_copy(
            sq_own, sq_in.at[k - 1], sq_sem.at[0, k - 1], sq_sem.at[1, k - 1],
            device_id={"tp": t_at(k)}, device_id_type=MESH,
        )

    def enter():
        below = (high > 1).astype(jnp.int32) + hears_far + (high > half + 1) + first_tail
        for n in range(4):

            @pl.when(below == n)
            def _():
                pl.semaphore_wait(barrier, partners + n)

        @pl.when(hears_far)
        def _():
            pl.semaphore_signal(
                far_ok, inc=1, device_id={"ctx": z_off(-2 * GROUP)}, device_id_type=MESH
            )

        for n, g in enumerate(beyond):

            @pl.when(high == g)
            def _():
                pl.semaphore_signal(
                    wrap_ok.at[n], inc=1, device_id={"ctx": low}, device_id_type=MESH
                )

        @pl.when(high > 1)
        def _():
            pl.semaphore_signal(
                up_ok, inc=1, device_id={"ctx": z_off(-GROUP)}, device_id_type=MESH
            )

        @pl.when(first_tail)
        def _():
            pl.semaphore_signal(
                first_ok, inc=1, device_id={"ctx": z_off(1)}, device_id_type=MESH
            )

    position = lax.broadcasted_iota(jnp.int32, (BLK, HEAD_DIM), 0).astype(f32)
    rate_copy.wait()
    for slot in order:
        rate = rate_of(slot)
        load(0, slot).wait()
        load(1, slot).wait()
        tail = jnp.exp(-rate * (BLK - position))
        block_decay = fixed_decay(rate, BLK)
        state = None
        for block in range(blocks):
            at = pl.ds(block * BLK, BLK)
            scaled = (k_buf[slot, at, :].astype(f32) * tail).astype(bf16)
            term = lax.dot_general(
                scaled, v_buf[slot, at, :], (((0,), (0,)), ((), ())), preferred_element_type=f32
            )
            if block < blocks - 1:
                first_term[slot, block] = term
            state = term if state is None else block_decay * state + term
        s_own[slot] = state.reshape(GROUP, slab, HEAD_DIM)

    enter()
    last_low = low == GROUP - 1
    slab_order = [jnp.where(last_low, 1, 3), 2, jnp.where(last_low, 3, 1), 0]
    for o in slab_order:
        for slot in order[:-1]:
            send_s(slot, o).start()

    line = lax.broadcasted_iota(jnp.int32, (BLK, BLK), 0)
    column = lax.broadcasted_iota(jnp.int32, (BLK, BLK), 1)
    causal = line >= column
    spread = jnp.maximum(line - column, 0).astype(f32)
    for slot in range(nx):
        load(2, slot).wait()
        weight = jnp.where(causal, jnp.exp(-rate_of(slot) * spread), 0.0)
        for block in range(blocks):
            at = pl.ds(block * BLK, BLK)
            scores = lax.dot_general(
                q_buf[slot, at, :], k_buf[slot, at, :], (((1,), (1,)), ((), ())),
                preferred_element_type=f32,
            )
            mixing = (scores * weight).astype(bf16)
            att[slot, at, :] = jnp.dot(mixing, v_buf[slot, at, :], preferred_element_type=f32)

    rate = rate_of(0)
    x_weight = [decay(rate, span * (nx - 1 - x_at(-k))) for k in range(nx)]
    z_span = span * nx
    z_weight = [decay(rate, z_span * (GROUP - 1 - low_at(-k))) for k in range(GROUP)]
    for n, o in enumerate(slab_order):
        plane = x_weight[0] * s_own[0, low_at(o)]
        for k in range(1, nx):
            send_s(k, o).wait_recv()
            plane = plane + x_weight[k] * s_in[k - 1, low_at(o)]
        t_own[o] = plane
        if n < GROUP - 1:
            send_t(o).start()

    @pl.when(second_head)
    def _():
        pl.semaphore_wait(first_ok, 1)
        for k in range(1, GROUP + 1):
            pl.semaphore_signal(up_ok, inc=1, device_id={"ctx": z_off(-k)}, device_id_type=MESH)

    x_entry = []
    for q in range(nx):
        goal = x_at(q)
        x_entry.append(decay(rate, span * goal))
        inner = [decay(rate, span * (goal - 1 - x_at(-j)), x_at(-j) < goal) for j in range(nx)]
        for k in range(GROUP):
            index = low_at(-k)
            value = inner[0] * s_own[0, index]
            for j in range(1, nx):
                value = value + inner[j] * s_in[j - 1, index]
            if q:
                px_out[q - 1, k] = value
            else:
                before[0, index] = value
    group_decay = fixed_decay(rate, z_span * GROUP)
    first_decay = decay(rate, z_span * GROUP * (high - 1))
    whole = z_weight[0] * t_own[0]
    for k in range(1, GROUP):
        send_t(k).wait_recv()
        whole = whole + z_weight[k] * t_in[k - 1]

    @pl.when(has_up)
    def _():
        pl.semaphore_wait(up_ok, 1)

    @pl.when(sends_far)
    def _():
        pl.semaphore_wait(far_ok, 1)

    @pl.when(sends_total)
    def _():
        up_out[...] = whole
        send_up().start()

    @pl.when(jnp.logical_not(has_down))
    def _():
        up_out[...] = whole
        send_first(up_out, 1, 0).start()
        first_in[...] = jnp.zeros_like(first_in)

    slabs = [t_own[0]] + [t_in[k - 1] for k in range(1, GROUP)]
    z_entry = []
    for k in range(GROUP):
        goal = low_at(k)
        z_entry.append(decay(rate, z_span * goal))
        value = None
        for j in range(GROUP):
            if (j + k) % GROUP:
                source = low_at(-j)
                term = decay(rate, z_span * (goal - 1 - source), source < goal) * slabs[j]
                value = term if value is None else value + term
        pz_out[k] = value

    @pl.when(high <= 1)
    def _():
        up_in[...] = jnp.zeros_like(up_in)

    @pl.when(high > 1)
    def _():
        send_up().wait_recv()

    @pl.when(takes_far)
    def _():
        send_far().wait_recv()
        up_in[...] = up_in[...] + group_decay * far_in[...]

    @pl.when(jnp.logical_and(chained, jnp.logical_not(sends_total)))
    def _():
        up_out[...] = whole + group_decay * up_in[...]

        @pl.when(sends_far)
        def _():
            send_far().start()

        send_up().start()

    @pl.when(has_down)
    def _():
        send_first(first_in, 1, 0).wait_recv()

    @pl.when(jnp.logical_and(relays_far, jnp.logical_not(sends_far)))
    def _():
        pl.semaphore_wait(far_ok, 1)

    @pl.when(relays_far)
    def _():
        send_first(first_in, 2, 1 + len(beyond)).start()

    @pl.when(relays)
    def _():
        send_first(first_in, 1, 0).start()

    incoming = up_in[...] + first_decay * first_in[...]

    for k in (3, 2, 1, 0):
        pz_out[k] = pz_out[k] + z_entry[k] * incoming
        if k:
            send_pz(k).start()

    for k in range(GROUP):
        if k:
            send_pz(k).wait_recv()
            base = pz_in[k - 1]
        else:
            base = pz_out[0]
        index = low_at(-k)
        for q in (2, 1, 3, 0):
            if q:
                px_out[q - 1, k] = px_out[q - 1, k] + x_entry[q] * base
                send_px(q, k).start()
            else:
                before[0, index] = before[0, index] + x_entry[0] * base

    squares = [jnp.zeros((BLK, HEAD_DIM), f32) for block in range(blocks)]
    for q in (0, 1, 3, 2):
        slot = (nx - q) % nx
        if q:
            for k in range(GROUP):
                pltpu.make_async_remote_copy(
                    px_out.at[q - 1, k], before.at[slot, low_at(-k)],
                    px_sem.at[0, q - 1, k], px_sem.at[1, q - 1, k],
                    device_id={"exp": x_at(q)}, device_id_type=MESH,
                ).wait_recv()
        rate = rate_of(slot)
        inner_decay = jnp.exp(-rate * position)
        block_decay = fixed_decay(rate, BLK)
        state = before[slot].reshape(HEAD_DIM, HEAD_DIM)
        for block in range(blocks):
            at = pl.ds(block * BLK, BLK)
            carried = jnp.dot(
                q_buf[slot, at, :], state.astype(bf16), preferred_element_type=f32
            )
            attended = att[slot, at, :] + carried * inner_decay
            att[slot, at, :] = attended
            squares[block] = squares[block] + attended * attended
            if block < blocks - 1:
                state = block_decay * state + first_term[slot, block]

    pieces = rows // HEAD_DIM
    per_block = BLK // HEAD_DIM
    for c in range(pieces):
        part = squares[c // per_block][(c % per_block) * HEAD_DIM : (c % per_block + 1) * HEAD_DIM]
        sq_own[pl.ds(c, 1), :] = jnp.sum(part.T, axis=0, keepdims=True)
    for k in range(1, nt):
        send_sq(k).start()
    sum_squares = sq_own[...]
    for k in range(1, nt):
        send_sq(k).wait_recv()
        sum_squares = sum_squares + sq_in[k - 1]
    gain_copy.wait()
    scale = lax.rsqrt(sum_squares / (nt * nx * HEAD_DIM) + 1e-06)
    for c in range(pieces):
        at = pl.ds(c * HEAD_DIM, HEAD_DIM)
        row_scale = jnp.broadcast_to(scale[c : c + 1], (HEAD_DIM, HEAD_DIM)).T
        for slot in range(nx):
            head = x_at(slot)
            lanes = pl.ds(pl.multiple_of(head * HEAD_DIM, HEAD_DIM), HEAD_DIM)
            gain = gain_ref[pl.ds(head, 1), :]
            out_ref[at, lanes] = (att[slot, at, :] * row_scale * gain).astype(bf16)

    for k in range(1, nx):
        for c in range(GROUP):
            send_s(k, c).wait_send()
            send_px(k, c).wait_send()
    for k in range(1, GROUP):
        send_t(k).wait_send()
        send_pz(k).wait_send()

    @pl.when(jnp.logical_not(has_down))
    def _():
        for n, g in enumerate(beyond):
            pl.semaphore_wait(wrap_ok.at[n], 1)
            send_first(up_out, g, 1 + n).start()
        send_first(up_out, 1, 0).wait_send()
        for n, g in enumerate(beyond):
            send_first(up_out, g, 1 + n).wait_send()

    @pl.when(relays)
    def _():
        send_first(first_in, 1, 0).wait_send()

    @pl.when(relays_far)
    def _():
        send_first(first_in, 2, 1 + len(beyond)).wait_send()

    @pl.when(chained)
    def _():
        send_up().wait_send()

    @pl.when(sends_far)
    def _():
        send_far().wait_send()

    for k in range(1, nt):
        send_sq(k).wait_send()


def solution(mesh):
    nz, nx, nt = mesh.shape["ctx"], mesh.shape["exp"], mesh.shape["tp"]
    slab = HEAD_DIM // GROUP
    groups = nz // GROUP
    beyond = max(groups - 2 - groups // 2, 1)

    def local(queries, key_vectors, value_vectors, decay_rate, norm_gain):
        rows, width = queries.shape
        heads = width // HEAD_DIM
        blocks = rows // BLK
        f32 = jnp.float32
        square = (HEAD_DIM, HEAD_DIM)
        piece = (slab, HEAD_DIM)
        dma = pltpu.SemaphoreType.DMA
        scratch = [
            pltpu.SMEM((heads,), f32),
            pltpu.VMEM((heads, HEAD_DIM), f32),
            pltpu.VMEM((heads, rows, HEAD_DIM), jnp.bfloat16),
            pltpu.VMEM((heads, rows, HEAD_DIM), jnp.bfloat16),
            pltpu.VMEM((heads, rows, HEAD_DIM), jnp.bfloat16),
            pltpu.VMEM((heads, rows, HEAD_DIM), f32),
            pltpu.VMEM((heads, max(blocks - 1, 1)) + square, f32),
            pltpu.VMEM((heads, GROUP) + piece, f32),
            pltpu.VMEM((nx - 1, GROUP) + piece, f32),
            pltpu.VMEM((GROUP,) + piece, f32),
            pltpu.VMEM((GROUP - 1,) + piece, f32),
            pltpu.VMEM(piece, f32),
            pltpu.VMEM(piece, f32),
            pltpu.VMEM(piece, f32),
            pltpu.VMEM(piece, f32),
            pltpu.VMEM((GROUP,) + piece, f32),
            pltpu.VMEM((GROUP - 1,) + piece, f32),
            pltpu.VMEM((nx - 1, GROUP) + piece, f32),
            pltpu.VMEM((heads, GROUP) + piece, f32),
            pltpu.VMEM((rows // HEAD_DIM, HEAD_DIM), f32),
            pltpu.VMEM((nt - 1, rows // HEAD_DIM, HEAD_DIM), f32),
            dma((3, heads)),
            dma,
            dma,
            pltpu.SemaphoreType.REGULAR,
            pltpu.SemaphoreType.REGULAR,
            pltpu.SemaphoreType.REGULAR((beyond,)),
            pltpu.SemaphoreType.REGULAR,
            dma((2, nx - 1, GROUP)),
            dma((2, GROUP - 1)),
            dma((4,)),
            dma((3 + beyond,)),
            dma((2, GROUP - 1)),
            dma((2, nx - 1, GROUP)),
            dma((2, nt - 1)),
        ]
        return pl.pallas_call(
            functools.partial(kernel, (nz, nx, nt)),
            out_shape=pltpu.VMEM((rows, width), jnp.bfloat16),
            in_specs=[
                pl.BlockSpec(memory_space=pl.ANY),
                pl.BlockSpec(memory_space=pl.ANY),
                pl.BlockSpec(memory_space=pl.ANY),
                pl.BlockSpec(memory_space=pl.ANY),
                pl.BlockSpec(memory_space=pl.ANY),
            ],
            out_specs=pl.BlockSpec(memory_space=pltpu.VMEM),
            scratch_shapes=scratch,
            compiler_params=pltpu.CompilerParams(collective_id=0, has_side_effects=True),
            name="lightning",
        )(queries, key_vectors, value_vectors, decay_rate, norm_gain.reshape(heads, HEAD_DIM))

    return jax.shard_map(
        local,
        mesh=mesh,
        in_specs=(
            P(("ctx", "exp"), "tp"),
            P(("ctx", "exp"), "tp"),
            P(("ctx", "exp"), "tp"),
            P("tp"),
            P("tp"),
        ),
        out_specs=P(("ctx", "exp"), "tp"),
        check_vma=False,
    )
```

```python
import functools

import jax
import jax.numpy as jnp
from jax import lax
from jax.experimental import pallas as pl
from jax.experimental.pallas import tpu as pltpu
from jax.sharding import PartitionSpec as P

HEADS = 32
HEAD_DIM = 128
BLK = 256
GROUP = 4
MESH = pl.DeviceIdType.MESH


def kernel(
    sizes,
    q_hbm,
    k_hbm,
    v_hbm,
    rate_hbm,
    gain_hbm,
    out_ref,
    rate_ref,
    gain_ref,
    q_buf,
    k_buf,
    v_buf,
    att,
    first_term,
    s_own,
    s_in,
    t_own,
    t_in,
    up_out,
    up_in,
    far_in,
    first_in,
    pz_out,
    pz_in,
    px_out,
    before,
    sq_own,
    sq_in,
    load_sem,
    rate_sem,
    gain_sem,
    up_ok,
    far_ok,
    wrap_ok,
    first_ok,
    s_sem,
    t_sem,
    up_sem,
    first_sem,
    pz_sem,
    px_sem,
    sq_sem,
):
    nz, nx, nt = sizes
    groups = nz // GROUP
    rows = q_hbm.shape[0]
    blocks = rows // BLK
    span = rows
    slab = HEAD_DIM // GROUP
    f32, bf16 = jnp.float32, jnp.bfloat16

    z, x, t = lax.axis_index("ctx"), lax.axis_index("exp"), lax.axis_index("tp")
    low = lax.rem(z, GROUP)
    high = lax.div(z, GROUP)

    def x_at(k):
        return lax.rem(x + (k + nx), nx)

    def low_at(k):
        return lax.rem(low + (k + GROUP), GROUP)

    def z_at(k):
        return z - low + low_at(k)

    def t_at(k):
        return lax.rem(t + k, nt)

    half = groups // 2
    odd = lax.rem(high, 2) == 1
    has_down, has_up = high > 0, high < groups - 1
    takes_far = jnp.logical_and(odd, high >= half + 1)
    chained = jnp.logical_and(high > 0, has_up)
    relays = jnp.logical_and(odd, high <= half)
    relays_far = jnp.logical_and(odd, high <= half - 1)
    hears_far = jnp.logical_and(odd, high >= 3)
    heard_far = jnp.logical_and(odd, high < groups - 2)
    first_tail = jnp.logical_and(high == 0, low == GROUP - 1)
    second_head = jnp.logical_and(high == 1, low == 0)
    beyond = list(range(groups - 1, half + 1, -1))
    sends_far = jnp.logical_and(odd, jnp.logical_and(high >= half - 1, high < groups - 2))
    sends_total = jnp.logical_and(jnp.logical_not(odd), high >= half)

    def z_off(k):
        return lax.rem(z + (k + nz), nz)

    barrier = pltpu.get_barrier_semaphore()
    partners = (GROUP - 1) + (nx - 1) + (nt - 1)

    @pl.when(heard_far)
    def _():
        pl.semaphore_signal(
            barrier, inc=1, device_id={"ctx": z_off(2 * GROUP)}, device_id_type=MESH
        )

    @pl.when(chained)
    def _():
        pl.semaphore_signal(barrier, inc=1, device_id={"ctx": z_off(GROUP)}, device_id_type=MESH)

    @pl.when(second_head)
    def _():
        pl.semaphore_signal(barrier, inc=1, device_id={"ctx": z_off(-1)}, device_id_type=MESH)

    @pl.when(high == 0)
    def _():
        for g in beyond:
            pl.semaphore_signal(
                barrier, inc=1, device_id={"ctx": z_off(GROUP * g)}, device_id_type=MESH
            )

    for k in range(1, GROUP):
        pl.semaphore_signal(barrier, inc=1, device_id={"ctx": z_at(k)}, device_id_type=MESH)
    for k in range(1, nx):
        pl.semaphore_signal(barrier, inc=1, device_id={"exp": x_at(k)}, device_id_type=MESH)
    for k in range(1, nt):
        pl.semaphore_signal(barrier, inc=1, device_id={"tp": t_at(k)}, device_id_type=MESH)

    def load(which, slot):
        source, target = ((k_hbm, k_buf), (v_hbm, v_buf), (q_hbm, q_buf))[which]
        lanes = pl.ds(pl.multiple_of(x_at(slot) * HEAD_DIM, HEAD_DIM), HEAD_DIM)
        return pltpu.make_async_copy(
            source.at[:, lanes], target.at[slot], load_sem.at[which, slot]
        )

    rate_copy = pltpu.make_async_copy(rate_hbm, rate_ref, rate_sem)
    gain_copy = pltpu.make_async_copy(gain_hbm, gain_ref, gain_sem)
    rate_copy.start()
    order = [2, 1, 3, 0] if nx == 4 else list(range(1, nx)) + [0]
    for slot in order:
        load(0, slot).start()
        load(1, slot).start()
    for slot in range(nx):
        load(2, slot).start()
    gain_copy.start()

    def rate_of(slot):
        return rate_ref[x_at(slot)]

    def decay(rate, distance, valid=None):
        distance = jnp.maximum(distance, 0)
        weight = jnp.exp(jnp.full((1, HEAD_DIM), -rate * distance.astype(f32), f32))
        if valid is not None:
            weight = weight * jnp.where(valid, 1.0, 0.0).astype(f32)
        return weight

    def fixed_decay(rate, distance):
        return jnp.exp(jnp.full((1, HEAD_DIM), -rate * float(distance), f32))

    def send_s(k, o):
        return pltpu.make_async_remote_copy(
            s_own.at[k, low_at(o)], s_in.at[k - 1, low_at(o)],
            s_sem.at[0, k - 1, o], s_sem.at[1, k - 1, o],
            device_id={"exp": x_at(k)}, device_id_type=MESH,
        )

    def send_t(k):
        return pltpu.make_async_remote_copy(
            t_own.at[k], t_in.at[k - 1], t_sem.at[0, k - 1], t_sem.at[1, k - 1],
            device_id={"ctx": z_at(k)}, device_id_type=MESH,
        )

    def send_up():
        return pltpu.make_async_remote_copy(
            up_out, up_in, up_sem.at[0], up_sem.at[1],
            device_id={"ctx": z_off(GROUP)}, device_id_type=MESH,
        )

    def send_far():
        return pltpu.make_async_remote_copy(
            up_out, far_in, up_sem.at[2], up_sem.at[3],
            device_id={"ctx": z_off(2 * GROUP)}, device_id_type=MESH,
        )

    def send_first(source, g, n):
        return pltpu.make_async_remote_copy(
            source, first_in, first_sem.at[1 + n], first_sem.at[0],
            device_id={"ctx": z_off(GROUP * g)}, device_id_type=MESH,
        )

    def send_pz(k):
        return pltpu.make_async_remote_copy(
            pz_out.at[k], pz_in.at[k - 1], pz_sem.at[0, k - 1], pz_sem.at[1, k - 1],
            device_id={"ctx": z_at(k)}, device_id_type=MESH,
        )

    def send_px(q, k):
        return pltpu.make_async_remote_copy(
            px_out.at[q - 1, k], before.at[nx - q, low_at(-k)],
            px_sem.at[0, q - 1, k], px_sem.at[1, q - 1, k],
            device_id={"exp": x_at(q)}, device_id_type=MESH,
        )

    def send_sq(k):
        return pltpu.make_async_remote_copy(
            sq_own, sq_in.at[k - 1], sq_sem.at[0, k - 1], sq_sem.at[1, k - 1],
            device_id={"tp": t_at(k)}, device_id_type=MESH,
        )

    def enter():
        below = (high > 1).astype(jnp.int32) + hears_far + (high > half + 1) + first_tail
        for n in range(4):

            @pl.when(below == n)
            def _():
                pl.semaphore_wait(barrier, partners + n)

        @pl.when(hears_far)
        def _():
            pl.semaphore_signal(
                far_ok, inc=1, device_id={"ctx": z_off(-2 * GROUP)}, device_id_type=MESH
            )

        for n, g in enumerate(beyond):

            @pl.when(high == g)
            def _():
                pl.semaphore_signal(
                    wrap_ok.at[n], inc=1, device_id={"ctx": low}, device_id_type=MESH
                )

        @pl.when(high > 1)
        def _():
            pl.semaphore_signal(
                up_ok, inc=1, device_id={"ctx": z_off(-GROUP)}, device_id_type=MESH
            )

        @pl.when(first_tail)
        def _():
            pl.semaphore_signal(
                first_ok, inc=1, device_id={"ctx": z_off(1)}, device_id_type=MESH
            )

    position = lax.broadcasted_iota(jnp.int32, (BLK, HEAD_DIM), 0).astype(f32)
    rate_copy.wait()
    for slot in order:
        rate = rate_of(slot)
        load(0, slot).wait()
        load(1, slot).wait()
        tail = jnp.exp(-rate * (BLK - position))
        block_decay = fixed_decay(rate, BLK)
        state = None
        for block in range(blocks):
            at = pl.ds(block * BLK, BLK)
            scaled = (k_buf[slot, at, :].astype(f32) * tail).astype(bf16)
            term = lax.dot_general(
                scaled, v_buf[slot, at, :], (((0,), (0,)), ((), ())), preferred_element_type=f32
            )
            if block < blocks - 1:
                first_term[slot, block] = term
            state = term if state is None else block_decay * state + term
        s_own[slot] = state.reshape(GROUP, slab, HEAD_DIM)

    enter()
    for o in (3, 2, 1, 0):
        for slot in order[:-1]:
            send_s(slot, o).start()

    line = lax.broadcasted_iota(jnp.int32, (BLK, BLK), 0)
    column = lax.broadcasted_iota(jnp.int32, (BLK, BLK), 1)
    causal = line >= column
    spread = jnp.maximum(line - column, 0).astype(f32)
    for slot in range(nx):
        load(2, slot).wait()
        weight = jnp.where(causal, jnp.exp(-rate_of(slot) * spread), 0.0)
        for block in range(blocks):
            at = pl.ds(block * BLK, BLK)
            scores = lax.dot_general(
                q_buf[slot, at, :], k_buf[slot, at, :], (((1,), (1,)), ((), ())),
                preferred_element_type=f32,
            )
            mixing = (scores * weight).astype(bf16)
            att[slot, at, :] = jnp.dot(mixing, v_buf[slot, at, :], preferred_element_type=f32)

    rate = rate_of(0)
    x_weight = [decay(rate, span * (nx - 1 - x_at(-k))) for k in range(nx)]
    z_span = span * nx
    z_weight = [decay(rate, z_span * (GROUP - 1 - low_at(-k))) for k in range(GROUP)]
    for o in (3, 2, 1, 0):
        plane = x_weight[0] * s_own[0, low_at(o)]
        for k in range(1, nx):
            send_s(k, o).wait_recv()
            plane = plane + x_weight[k] * s_in[k - 1, low_at(o)]
        t_own[o] = plane
        if o:
            send_t(o).start()

    @pl.when(second_head)
    def _():
        pl.semaphore_wait(first_ok, 1)
        for k in range(1, GROUP + 1):
            pl.semaphore_signal(up_ok, inc=1, device_id={"ctx": z_off(-k)}, device_id_type=MESH)

    x_entry = []
    for q in range(nx):
        goal = x_at(q)
        x_entry.append(decay(rate, span * goal))
        inner = [decay(rate, span * (goal - 1 - x_at(-j)), x_at(-j) < goal) for j in range(nx)]
        for k in range(GROUP):
            index = low_at(-k)
            value = inner[0] * s_own[0, index]
            for j in range(1, nx):
                value = value + inner[j] * s_in[j - 1, index]
            if q:
                px_out[q - 1, k] = value
            else:
                before[0, index] = value
    group_decay = fixed_decay(rate, z_span * GROUP)
    first_decay = decay(rate, z_span * GROUP * (high - 1))
    whole = z_weight[0] * t_own[0]
    for k in range(1, GROUP):
        send_t(k).wait_recv()
        whole = whole + z_weight[k] * t_in[k - 1]

    @pl.when(has_up)
    def _():
        pl.semaphore_wait(up_ok, 1)

    @pl.when(sends_far)
    def _():
        pl.semaphore_wait(far_ok, 1)

    @pl.when(sends_total)
    def _():
        up_out[...] = whole
        send_up().start()

    @pl.when(jnp.logical_not(has_down))
    def _():
        up_out[...] = whole
        send_first(up_out, 1, 0).start()
        first_in[...] = jnp.zeros_like(first_in)

    slabs = [t_own[0]] + [t_in[k - 1] for k in range(1, GROUP)]
    z_entry = []
    for k in range(GROUP):
        goal = low_at(k)
        z_entry.append(decay(rate, z_span * goal))
        value = None
        for j in range(GROUP):
            if (j + k) % GROUP:
                source = low_at(-j)
                term = decay(rate, z_span * (goal - 1 - source), source < goal) * slabs[j]
                value = term if value is None else value + term
        pz_out[k] = value

    @pl.when(high <= 1)
    def _():
        up_in[...] = jnp.zeros_like(up_in)

    @pl.when(high > 1)
    def _():
        send_up().wait_recv()

    @pl.when(takes_far)
    def _():
        send_far().wait_recv()
        up_in[...] = up_in[...] + group_decay * far_in[...]

    @pl.when(jnp.logical_and(chained, jnp.logical_not(sends_total)))
    def _():
        up_out[...] = whole + group_decay * up_in[...]

        @pl.when(sends_far)
        def _():
            send_far().start()

        send_up().start()

    @pl.when(has_down)
    def _():
        send_first(first_in, 1, 0).wait_recv()

    @pl.when(jnp.logical_and(relays_far, jnp.logical_not(sends_far)))
    def _():
        pl.semaphore_wait(far_ok, 1)

    @pl.when(relays_far)
    def _():
        send_first(first_in, 2, 1 + len(beyond)).start()

    @pl.when(relays)
    def _():
        send_first(first_in, 1, 0).start()

    incoming = up_in[...] + first_decay * first_in[...]

    for k in (3, 2, 1, 0):
        pz_out[k] = pz_out[k] + z_entry[k] * incoming
        if k:
            send_pz(k).start()

    for k in range(GROUP):
        if k:
            send_pz(k).wait_recv()
            base = pz_in[k - 1]
        else:
            base = pz_out[0]
        index = low_at(-k)
        for q in (2, 1, 3, 0):
            if q:
                px_out[q - 1, k] = px_out[q - 1, k] + x_entry[q] * base
                send_px(q, k).start()
            else:
                before[0, index] = before[0, index] + x_entry[0] * base

    squares = [jnp.zeros((BLK, HEAD_DIM), f32) for block in range(blocks)]
    for q in (0, 1, 3, 2):
        slot = (nx - q) % nx
        if q:
            for k in range(GROUP):
                pltpu.make_async_remote_copy(
                    px_out.at[q - 1, k], before.at[slot, low_at(-k)],
                    px_sem.at[0, q - 1, k], px_sem.at[1, q - 1, k],
                    device_id={"exp": x_at(q)}, device_id_type=MESH,
                ).wait_recv()
        rate = rate_of(slot)
        inner_decay = jnp.exp(-rate * position)
        block_decay = fixed_decay(rate, BLK)
        state = before[slot].reshape(HEAD_DIM, HEAD_DIM)
        for block in range(blocks):
            at = pl.ds(block * BLK, BLK)
            carried = jnp.dot(
                q_buf[slot, at, :], state.astype(bf16), preferred_element_type=f32
            )
            attended = att[slot, at, :] + carried * inner_decay
            att[slot, at, :] = attended
            squares[block] = squares[block] + attended * attended
            if block < blocks - 1:
                state = block_decay * state + first_term[slot, block]

    pieces = rows // HEAD_DIM
    per_block = BLK // HEAD_DIM
    ones = jnp.ones((8, HEAD_DIM), bf16)
    across = (((1,), (1,)), ((), ()))
    for block in range(blocks):
        high_part = squares[block].astype(bf16)
        low_part = (squares[block] - high_part.astype(f32)).astype(bf16)
        sums = lax.dot_general(ones, high_part, across, preferred_element_type=f32)
        sums = sums + lax.dot_general(ones, low_part, across, preferred_element_type=f32)
        for c in range(per_block):
            sq_own[pl.ds(block * per_block + c, 1), :] = sums[
                :1, c * HEAD_DIM : (c + 1) * HEAD_DIM
            ]
    for k in range(1, nt):
        send_sq(k).start()
    gain_copy.wait()
    for slot in range(nx):
        att[slot] = att[slot] * gain_ref[pl.ds(x_at(slot), 1), :]
    sum_squares = sq_own[...]
    for k in range(1, nt):
        send_sq(k).wait_recv()
        sum_squares = sum_squares + sq_in[k - 1]
    scale = lax.rsqrt(sum_squares / (nt * nx * HEAD_DIM) + 1e-06)
    for c in range(pieces):
        at = pl.ds(c * HEAD_DIM, HEAD_DIM)
        row_scale = jnp.broadcast_to(scale[c : c + 1], (HEAD_DIM, HEAD_DIM)).T
        for slot in range(nx):
            head = x_at(slot)
            lanes = pl.ds(pl.multiple_of(head * HEAD_DIM, HEAD_DIM), HEAD_DIM)
            out_ref[at, lanes] = (att[slot, at, :] * row_scale).astype(bf16)

    for k in range(1, nx):
        for c in range(GROUP):
            send_s(k, c).wait_send()
            send_px(k, c).wait_send()
    for k in range(1, GROUP):
        send_t(k).wait_send()
        send_pz(k).wait_send()

    @pl.when(jnp.logical_not(has_down))
    def _():
        for n, g in enumerate(beyond):
            pl.semaphore_wait(wrap_ok.at[n], 1)
            send_first(up_out, g, 1 + n).start()
        send_first(up_out, 1, 0).wait_send()
        for n, g in enumerate(beyond):
            send_first(up_out, g, 1 + n).wait_send()

    @pl.when(relays)
    def _():
        send_first(first_in, 1, 0).wait_send()

    @pl.when(relays_far)
    def _():
        send_first(first_in, 2, 1 + len(beyond)).wait_send()

    @pl.when(chained)
    def _():
        send_up().wait_send()

    @pl.when(sends_far)
    def _():
        send_far().wait_send()

    for k in range(1, nt):
        send_sq(k).wait_send()


def solution(mesh):
    nz, nx, nt = mesh.shape["ctx"], mesh.shape["exp"], mesh.shape["tp"]
    slab = HEAD_DIM // GROUP
    groups = nz // GROUP
    beyond = max(groups - 2 - groups // 2, 1)

    def local(queries, key_vectors, value_vectors, decay_rate, norm_gain):
        rows, width = queries.shape
        heads = width // HEAD_DIM
        blocks = rows // BLK
        f32 = jnp.float32
        square = (HEAD_DIM, HEAD_DIM)
        piece = (slab, HEAD_DIM)
        dma = pltpu.SemaphoreType.DMA
        scratch = [
            pltpu.SMEM((heads,), f32),
            pltpu.VMEM((heads, HEAD_DIM), f32),
            pltpu.VMEM((heads, rows, HEAD_DIM), jnp.bfloat16),
            pltpu.VMEM((heads, rows, HEAD_DIM), jnp.bfloat16),
            pltpu.VMEM((heads, rows, HEAD_DIM), jnp.bfloat16),
            pltpu.VMEM((heads, rows, HEAD_DIM), f32),
            pltpu.VMEM((heads, max(blocks - 1, 1)) + square, f32),
            pltpu.VMEM((heads, GROUP) + piece, f32),
            pltpu.VMEM((nx - 1, GROUP) + piece, f32),
            pltpu.VMEM((GROUP,) + piece, f32),
            pltpu.VMEM((GROUP - 1,) + piece, f32),
            pltpu.VMEM(piece, f32),
            pltpu.VMEM(piece, f32),
            pltpu.VMEM(piece, f32),
            pltpu.VMEM(piece, f32),
            pltpu.VMEM((GROUP,) + piece, f32),
            pltpu.VMEM((GROUP - 1,) + piece, f32),
            pltpu.VMEM((nx - 1, GROUP) + piece, f32),
            pltpu.VMEM((heads, GROUP) + piece, f32),
            pltpu.VMEM((rows // HEAD_DIM, HEAD_DIM), f32),
            pltpu.VMEM((nt - 1, rows // HEAD_DIM, HEAD_DIM), f32),
            dma((3, heads)),
            dma,
            dma,
            pltpu.SemaphoreType.REGULAR,
            pltpu.SemaphoreType.REGULAR,
            pltpu.SemaphoreType.REGULAR((beyond,)),
            pltpu.SemaphoreType.REGULAR,
            dma((2, nx - 1, GROUP)),
            dma((2, GROUP - 1)),
            dma((4,)),
            dma((3 + beyond,)),
            dma((2, GROUP - 1)),
            dma((2, nx - 1, GROUP)),
            dma((2, nt - 1)),
        ]
        return pl.pallas_call(
            functools.partial(kernel, (nz, nx, nt)),
            out_shape=pltpu.VMEM((rows, width), jnp.bfloat16),
            in_specs=[
                pl.BlockSpec(memory_space=pl.ANY),
                pl.BlockSpec(memory_space=pl.ANY),
                pl.BlockSpec(memory_space=pl.ANY),
                pl.BlockSpec(memory_space=pl.ANY),
                pl.BlockSpec(memory_space=pl.ANY),
            ],
            out_specs=pl.BlockSpec(memory_space=pltpu.VMEM),
            scratch_shapes=scratch,
            compiler_params=pltpu.CompilerParams(collective_id=0, has_side_effects=True),
            name="lightning",
        )(queries, key_vectors, value_vectors, decay_rate, norm_gain.reshape(heads, HEAD_DIM))

    return jax.shard_map(
        local,
        mesh=mesh,
        in_specs=(
            P(("ctx", "exp"), "tp"),
            P(("ctx", "exp"), "tp"),
            P(("ctx", "exp"), "tp"),
            P("tp"),
            P("tp"),
        ),
        out_specs=P(("ctx", "exp"), "tp"),
        check_vma=False,
    )
```
